32 devices in a mesh: row: 8 (over y, x, core), col: 4 (over z).
Axes of the slice: x: 2, y: 2, z: 4, core: 2. Of those that a mesh axis runs over, the one named last changes fastest.
Arguments:
- screened: bfloat16 [16384, 16384], P('row', 'col'), may hold values from -0.046875 to 0.046875
- val_orbitals: bfloat16 [45, 16384], P(None, 'col'), may hold values from -6 to 6
- con_orbitals: bfloat16 [64, 16384], replicated, may hold values from -6 to 6
- val_pairs: int32 [1024, 2], replicated, may hold values from 0 to 44, as said below
- con_pairs: int32 [4096, 2], replicated, may hold values from 0 to 63
Outputs:
- kernel: float32 [4096, 1024], P('row', 'col')
The draws below stay inside these ranges and needn't reach their ends.
Inputs may be any that keep to these rules, and one draw needn't show every extreme that they name: `val_pairs`: each row holds v <= v'.
All inputs are finite; a program needn't handle non-finite values.
Results may differ from the reference program's by a relative error of at most 0.0049.
Values may be sent and summed in bfloat16 or wider, within the bound.
No kernel may reach another device: no remote copies, remote signals or barrier semaphores. Data moves between devices by JAX's collectives and lax.ppermute only.
A program may use at most 128 MiB of HBM per device.

```python
import jax
import jax.numpy as jnp

NG = 16384
NVB = 45
NCB = 64
NVP = 1024
NCP = 4096


def draw_val_pairs(key, part):
    first = jax.random.randint(jax.random.fold_in(key, 11), (NVP,), 0, NVB)
    second = jax.random.randint(jax.random.fold_in(key, 12), (NVP,), 0, NVB)
    return jnp.stack([jnp.minimum(first, second), jnp.maximum(first, second)], axis=1).astype(jnp.int32)


def place_ends(result, rng, smallest, high):
    extent = result.shape
    spot = [jax.random.randint(jax.random.fold_in(rng, axis), (), 0, extent[axis]) for axis in range(len(extent))]
    result = result.at[tuple(spot)].set(smallest)
    longest = extent.index(max(extent))
    spot[longest] = (spot[longest] + 1) % extent[longest]
    return result.at[tuple(spot)].set(high)


def steps_of(stream_key, dims, shards, low, top_value):
    def one(position, blocks):
        heights = jax.random.uniform(jax.random.fold_in(jax.random.fold_in(stream_key, 6), position), (blocks,), jnp.float32, low / len(shards), top_value / len(shards))
        return jnp.repeat(jnp.exp(heights), dims[position] // blocks).reshape((-1,) + (1,) * (len(dims) - position - 1))

    level = one(*shards[0])
    for cut in shards[1:]:
        level = level * one(*cut)
    return level


def scatter_about(own_key, extent, scale, bound, split=(), held_as=jnp.bfloat16):
    entries = scale * jax.random.normal(own_key, extent, jnp.float32)
    if split:
        entries = entries * steps_of(own_key, extent, split, -0.22, 0.18)
    return jnp.clip(entries, -bound, bound).astype(held_as)


def setup_inputs(seed: int = 0) -> dict:
    key_list = jax.random.split(jax.random.key(seed), 6)
    return {
        "screened": scatter_about(key_list[0], (NG, NG), NG ** -0.5, 0.046875, ((0, 8), (1, 4))),
        "val_orbitals": scatter_about(key_list[1], (NVB, NG), 1.0, 6.0, ((1, 4),)),
        "con_orbitals": scatter_about(key_list[2], (NCB, NG), 1.0, 6.0),
        "val_pairs": draw_val_pairs(jax.random.fold_in(key_list[5], 71), 0),
        "con_pairs": place_ends(jax.random.randint(key_list[4], (NCP, 2), 0, NCB), jax.random.fold_in(key_list[4], 1), 0, NCB - 1).astype(jnp.int32),
    }


def densities(orbitals, pairs):
    first = orbitals[pairs[:, 0]].astype(jnp.float32)
    second = orbitals[pairs[:, 1]].astype(jnp.float32)
    return (first * second).astype(jnp.bfloat16)


def reference(screened, val_orbitals, con_orbitals, val_pairs, con_pairs):
    val_density = densities(val_orbitals, val_pairs)
    screened_val = jnp.dot(screened, val_density.T, preferred_element_type=jnp.float32).astype(jnp.bfloat16)
    con_density = densities(con_orbitals, con_pairs)
    kernel = jnp.dot(con_density, screened_val, preferred_element_type=jnp.float32)
    return kernel * jnp.float32(NG ** -0.5)
```

```python
import jax
import jax.numpy as jnp
from jax import lax
from jax.sharding import PartitionSpec as P

CHUNKS = 4


def one_hot_rows(index, count):
    numbers = lax.broadcasted_iota(jnp.int32, (1, count), 1)
    return (index[:, None] == numbers).astype(jnp.bfloat16)


def densities(orbitals, first, second):
    count = orbitals.shape[0]
    a = jnp.dot(one_hot_rows(first, count), orbitals, preferred_element_type=jnp.float32)
    b = jnp.dot(one_hot_rows(second, count), orbitals, preferred_element_type=jnp.float32)
    return (a * b).astype(jnp.bfloat16)


def unordered_pairs(count):
    row = jnp.arange((count // 2 + 1) * count, dtype=jnp.int32)
    first = row % count
    return first, (first + row // count) % count


def unordered_row(pairs, count):
    c, other = pairs[:, 0], pairs[:, 1]
    apart = jnp.where(other >= c, other - c, other - c + count)
    return jnp.where(apart <= count // 2, apart * count + c, (count - apart) * count + other)


def halve(part, axis, bit, size):
    rows = part.shape[0] // 2
    mine = (lax.axis_index(axis) >> bit) & 1
    sent = lax.dynamic_slice_in_dim(part, (1 - mine) * rows, rows, 0).astype(jnp.bfloat16)
    kept = lax.dynamic_slice_in_dim(part, mine * rows, rows, 0)
    got = lax.ppermute(sent, axis, [(i, i ^ (1 << bit)) for i in range(size)])
    return kept + got.astype(jnp.float32)


def double(part, axis, bit, size):
    mine = (lax.axis_index(axis) >> bit) & 1
    got = lax.ppermute(part, axis, [(i, i ^ (1 << bit)) for i in range(size)])
    return jnp.where(mine == 0, jnp.concatenate([part, got]), jnp.concatenate([got, part]))


def solution(mesh):
    n_row, n_col = mesh.shape["row"], mesh.shape["col"]
    row_bits, col_bits = n_row.bit_length() - 1, n_col.bit_length() - 1

    def per_device(screened, val_orbitals, con_orbitals, val_pairs, con_pairs):
        own_rows, grid = screened.shape[0], con_orbitals.shape[1]
        count = con_orbitals.shape[0]
        n_pairs = val_pairs.shape[0]
        chunks = max(1, min(CHUNKS, n_pairs // (n_row * n_col)))
        width = n_pairs // n_col // chunks
        me = lax.axis_index("row")
        con_columns = lax.dynamic_slice_in_dim(con_orbitals, me * own_rows, own_rows, 1)
        con_density = densities(con_columns, *unordered_pairs(count))
        own = con_pairs.shape[0] // n_row
        asked = lax.dynamic_slice_in_dim(con_pairs, me * own, own, 0)
        pick = one_hot_rows(unordered_row(asked, count), con_density.shape[0])

        by_chunk = val_pairs.reshape(n_col, chunks, width, 2)
        results = []
        for k in range(chunks):
            order = [0] + (list(range(1, row_bits)) if k % 2 == 0 else list(range(row_bits - 1, 0, -1)))
            pairs = by_chunk[:, k].reshape(n_col, n_row, width // n_row, 2).transpose(1, 0, 2, 3)
            pairs = pairs.reshape(n_col * width, 2)
            val_density = densities(val_orbitals, pairs[:, 0], pairs[:, 1])
            screened_val = lax.dot_general(
                screened, val_density, (((1,), (1,)), ((), ())), preferred_element_type=jnp.float32
            ).astype(jnp.bfloat16)
            part = lax.dot_general(
                screened_val, con_density, (((0,), (1,)), ((), ())), preferred_element_type=jnp.float32
            )
            for bit in order:
                part = halve(part, "row", bit, n_row)
            for bit in reversed(range(col_bits)):
                part = halve(part, "col", bit, n_col)
            part = part.astype(jnp.bfloat16)
            for bit in reversed(order):
                part = double(part, "row", bit, n_row)
            results.append(part)
        whole = jnp.concatenate(results)
        kernel = lax.dot_general(
            pick, whole, (((1,), (1,)), ((), ())), preferred_element_type=jnp.float32
        )
        return kernel * jnp.float32(grid ** (-0.5))

    in_specs = (P("row", "col"), P(None, "col"), P(), P(), P())
    return jax.shard_map(
        per_device, mesh=mesh, in_specs=in_specs, out_specs=P("row", "col"), check_vma=False
    )
```

```python
import functools

import jax
import jax.numpy as jnp
from jax import lax
from jax.experimental import pallas as pl
from jax.experimental.pallas import tpu as pltpu
from jax.sharding import PartitionSpec as P


SHARES = (4, 2, 2)

F32, BF16 = jnp.float32, jnp.bfloat16
CONTRACT_MINOR = (((1,), (1,)), ((), ()))


def one_hot_columns(index, count):
    numbers = lax.broadcasted_iota(jnp.int32, (count, index.shape[1]), 0)
    return jnp.where(numbers == index, 1.0, 0.0)


def groups(ref, n_col, start, width):
    each = ref.shape[0] // n_col
    return jnp.concatenate([ref[z * each + start : z * each + start + width, :] for z in range(n_col)])


def build_val(first, second, val_ref, val_density):
    grid = val_ref.shape[1]
    step = min(2048, grid)

    @pl.loop(0, grid // step)
    def _(i):
        at = pl.ds(pl.multiple_of(i * step, step), step)
        orbitals = val_ref[:, at]
        a = jnp.dot(first, orbitals, preferred_element_type=F32)
        b = jnp.dot(second, orbitals, preferred_element_type=F32)
        val_density[:, at] = (a * b).astype(BF16)


def build_con(con, rolled, density):
    count, columns = con.shape
    wide = min(512, columns)
    apart = density.shape[0] // count

    @pl.loop(0, columns // wide)
    def _(i):
        at = pl.ds(pl.multiple_of(i * wide, wide), wide)
        one = con[:, at].astype(F32)
        for shift in range(8):
            moved = one if shift == 0 else jnp.concatenate([one[shift:], one[:shift]])
            rolled[0:count, :] = moved
            rolled[count : 2 * count, :] = moved
            for d in range(shift, apart, 8):
                other = rolled[d - shift : d - shift + count, :]
                density[d * count : (d + 1) * count, at] = (one * other).astype(BF16)


def product(numbers, w, density, val_density):
    stripe = w[0].shape[0]
    t = [lax.dot_general(val_density[...], w[s][...], CONTRACT_MINOR, preferred_element_type=F32).astype(BF16) for s in numbers]
    rows = slice(numbers[0] * stripe, (numbers[-1] + 1) * stripe)
    return lax.dot_general(jnp.concatenate(t, axis=1), density[:, rows], CONTRACT_MINOR, preferred_element_type=F32)


def hand_out(n_col, mine, acc, kept, sent):
    half = acc.shape[0] // n_col // 2
    for z in range(n_col):
        to = slice(z * half, (z + 1) * half)
        kept[to, :] = acc[pl.ds(pl.multiple_of((2 * z + mine) * half, half), half), :]
        sent[to, :] = acc[pl.ds(pl.multiple_of((2 * z + 1 - mine) * half, half), half), :].astype(BF16)


def first_kernel(n_col, width, n_stripes, place, pairs, val, con_all, w_hbm, kept, sent, *refs):
    w, refs = refs[:n_stripes], refs[n_stripes:]
    density, hot1, hot2, val_density, acc, pairs_here, val_here, con, rolled, sems, in_sems = refs
    me = place[0] // n_col
    columns, stripe = con.shape[1], w[0].shape[0]
    fetches = [
        pltpu.make_async_copy(pairs, pairs_here, in_sems.at[0]),
        pltpu.make_async_copy(val, val_here, in_sems.at[1]),
        pltpu.make_async_copy(
            con_all.at[:, pl.ds(pl.multiple_of(me * columns, columns), columns)], con, in_sems.at[2]
        ),
    ]
    for fetch in fetches:
        fetch.start()
    copies = []
    for s in range(n_stripes):
        copies.append(pltpu.make_async_copy(w_hbm.at[pl.ds(s * stripe, stripe), :], w[s], sems.at[s]))
        copies[-1].start()
    fetches[0].wait()
    hot1[...] = one_hot_columns(pairs_here[0:1, :], hot1.shape[1]).T.astype(BF16)
    hot2[...] = one_hot_columns(pairs_here[1:2, :], hot2.shape[1]).T.astype(BF16)
    fetches[1].wait()
    build_val(groups(hot1, n_col, 0, width), groups(hot2, n_col, 0, width), val_here, val_density)
    fetches[2].wait()
    build_con(con, rolled, density)
    for s, copy in enumerate(copies):
        copy.wait()
        part = product([s], w, density, val_density)
        if s == 0:
            acc[...] = part
        else:
            acc[...] += part
    hand_out(n_col, me % 2, acc, kept, sent)


def begin_kernel(n_col, start, width, n_stripes, numbers, n_after, *refs):
    w, refs = refs[:n_stripes], refs[n_stripes:]
    (density, hot1, hot2, val), refs = refs[:4], refs[4:]
    acc, val_density, *_ = refs[n_after:]
    build_val(groups(hot1, n_col, start, width), groups(hot2, n_col, start, width), val, val_density)
    acc[...] = product(numbers, w, density, val_density)


def end_kernel(n_col, n_stripes, numbers, n_after, place, *refs):
    w, refs = refs[:n_stripes], refs[n_stripes:]
    (density, before, val_density), refs = refs[:3], refs[3:]
    kept, sent, place_out, acc = *refs[n_after : n_after + 3], refs[-1]
    acc[...] = before[...] + product(numbers, w, density, val_density)
    hand_out(n_col, place[0] // n_col % 2, acc, kept, sent)
    place_out[0] = place[0]


def fold_kernel(n_col, bit, place, kept, got, kept_out, sent_out):
    high = ((place[0] // n_col) >> bit) % 2 == 1
    half = kept_out.shape[0] // n_col
    for z in range(n_col):
        a = slice(2 * z * half, (2 * z + 1) * half)
        b = slice((2 * z + 1) * half, (2 * z + 2) * half)
        to = slice(z * half, (z + 1) * half)
        low_part = kept[a, :] + got[a, :].astype(F32)
        high_part = kept[b, :] + got[b, :].astype(F32)
        kept_out[to, :] = jnp.where(high, high_part, low_part)
        sent_out[to, :] = jnp.where(high, low_part, high_part).astype(BF16)


def pick_kernel(n_col, count, scale, place, pairs, whole, out):
    own = out.shape[0]
    me = place[0] // n_col
    if own % 128:
        every = pairs[...]
        asked = functools.reduce(
            lambda a, i: jnp.where(me == i, every[:, i * own : (i + 1) * own], a), range(pairs.shape[1] // own), every[:, :own]
        )
    else:
        asked = pairs[:, pl.ds(pl.multiple_of(me * own, own), own)]
    c, other = asked[0:1], asked[1:2]
    apart = jnp.where(other >= c, other - c, other - c + count)
    row = jnp.where(apart <= count // 2, apart * count + c, (count - apart) * count + other)
    pick = one_hot_columns(row, whole.shape[1]).astype(BF16)
    out[...] = (jnp.dot(whole[...], pick, preferred_element_type=F32) * scale).T


def swap(x, axis, bit, size):
    return lax.ppermute(x, axis, [(i, i ^ (1 << bit)) for i in range(size)])


def solution(mesh):
    n_row, n_col = mesh.shape["row"], mesh.shape["col"]
    row_bits, col_bits = n_row.bit_length() - 1, n_col.bit_length() - 1

    def per_device(screened, val_orbitals, con_orbitals, val_pairs, con_pairs):
        own_rows, own_columns = screened.shape
        count, grid = con_orbitals.shape
        n_val = val_orbitals.shape[0]
        blocks = count // 2 + 1
        while blocks * count % 128:
            blocks += 1
        unordered = blocks * count
        n_pairs = val_pairs.shape[0]
        per_col = n_pairs // n_col
        shares = SHARES if n_pairs >= 32 * n_row * n_col else (8,)
        widths = [per_col * s // 8 for s in shares]
        starts = [sum(widths[:k]) for k in range(len(widths))]
        place = (lax.axis_index("row") * n_col + lax.axis_index("col")).astype(jnp.int32)[None]
        smem = pl.BlockSpec(memory_space=pltpu.SMEM)
        vmem = pl.BlockSpec(memory_space=pltpu.VMEM)
        anywhere = pl.BlockSpec(memory_space=pl.ANY)
        hbm = pl.BlockSpec(memory_space=pltpu.HBM)

        def params(mib):
            return pltpu.CompilerParams(vmem_limit_bytes=mib << 20)

        def cost(n, rows):
            return pl.CostEstimate(
                flops=2 * n * rows * (own_columns + unordered), bytes_accessed=1 << 20, transcendentals=0
            )

        def outs(rows):
            return [pltpu.VMEM((rows, unordered), F32), pltpu.VMEM((rows, unordered), BF16)]

        stripe = min(512, own_rows)
        hots = [pltpu.VMEM((n_pairs, n_val), BF16)] * 2
        n = n_col * widths[0]
        n_stripes = own_rows // stripe
        held = [pltpu.VMEM((stripe, own_columns), BF16)] * n_stripes + [pltpu.VMEM((unordered, own_rows), BF16)]
        n_held = n_stripes + 1
        kept, sent, *fixed = pl.pallas_call(
            functools.partial(first_kernel, n_col, widths[0], n_stripes),
            in_specs=[smem] + [hbm] * 4,
            out_specs=[vmem] * (2 + n_held + 2),
            out_shape=outs(n // 2) + held + hots,
            scratch_shapes=[
                pltpu.VMEM((n, own_columns), BF16),
                pltpu.VMEM((n, unordered), F32),
                pltpu.VMEM((2, n_pairs), jnp.int32),
                pltpu.VMEM((n_val, own_columns), BF16),
                pltpu.VMEM((count, own_rows), BF16),
                pltpu.VMEM((2 * count, min(512, own_rows)), F32),
                pltpu.SemaphoreType.DMA((n_stripes,)),
                pltpu.SemaphoreType.DMA((3,)),
            ],
            compiler_params=params(18),
            cost_estimate=cost(n, own_rows),
            name="first",
        )(place, *[pltpu.with_memory_space_constraint(x, pltpu.HBM) for x in (val_pairs.T, val_orbitals, con_orbitals, screened)])

        def begin(k, numbers, fixed, after):
            n = n_col * widths[k]
            acc, val_density, *fixed = pl.pallas_call(
                functools.partial(begin_kernel, n_col, starts[k], widths[k], n_stripes, numbers, len(after)),
                in_specs=[vmem] * (n_held + 3) + [anywhere] * len(after),
                out_specs=[vmem] * (2 + n_held + 2),
                out_shape=[pltpu.VMEM((n, unordered), F32), pltpu.VMEM((n, own_columns), BF16)] + held + hots,
                input_output_aliases={i: 2 + i for i in range(n_held + 2)},
                compiler_params=params(7),
                cost_estimate=cost(n, len(numbers) * stripe),
            )(*fixed, val_orbitals, *after)
            return (acc, val_density), fixed

        def end(k, numbers, fixed, before, after):
            n = n_col * widths[k]
            kept, sent, last_place, *same = pl.pallas_call(
                functools.partial(end_kernel, n_col, n_stripes, numbers, len(after)),
                in_specs=[smem] + [vmem] * (n_held + 2) + [anywhere] * len(after),
                out_specs=[vmem] * 2 + [smem] + [vmem] * n_held,
                out_shape=outs(n // 2) + [jax.ShapeDtypeStruct((1,), jnp.int32)] + held,
                scratch_shapes=[pltpu.VMEM((n, unordered), F32)],
                input_output_aliases={1 + i: 3 + i for i in range(n_held)},
                compiler_params=params(9),
                cost_estimate=cost(n, len(numbers) * stripe),
            )(place, *fixed[:n_held], *before, *after)
            return (kept, sent), last_place, same + fixed[n_held:]

        def fold(kept, got, bit):
            return pl.pallas_call(
                functools.partial(fold_kernel, n_col, bit),
                in_specs=[smem] + [vmem] * 2,
                out_specs=[vmem] * 2,
                out_shape=outs(kept.shape[0] // 2),
                compiler_params=params(4),
            )(place, kept, got)

        def step(k, at, kept, sent):
            got = swap(sent, "row", orders[k][at - 1], n_row)
            return fold(kept, got, orders[k][at])

        order = list(range(1, row_bits))
        orders = [[0] + (order if k % 2 == 0 else order[::-1]) for k in range(len(shares))]
        if len(shares) > 1:
            low, high = list(range(n_stripes // 2)), list(range(n_stripes // 2, n_stripes))
            a = kept, sent
            before, fixed = begin(1, low, fixed, [a[1]])
            a = step(0, 1, *a)
            b, last_place, fixed = end(1, high, fixed, before, [a[1]])
            before, fixed = begin(2, low, fixed, [b[1]])
            b = step(1, 1, *b)
            c, last_place, fixed = end(2, high, fixed, before, [b[1]])
            state = [(2, a), (2, b), (1, c)]
        else:
            last_place = place
            state = [(1, (kept, sent))]

        me = last_place[0]
        row, col = me // n_col, me % n_col

        def split(part, where, bit, each):
            size = part.shape[0] // (2 * each)
            mine = (where >> bit) & 1
            part = part.reshape(each, 2, size, unordered)
            take = lambda i: lax.dynamic_slice(
                part, (0, i, 0, 0), (each, 1, size, unordered), allow_negative_indices=False
            ).reshape(each * size, unordered)
            return take(mine), take(1 - mine).astype(BF16)

        def over_row(k, at, kept, sent):
            for at in range(at, row_bits + 1):
                part = kept + swap(sent, "row", orders[k][at - 1], n_row).astype(F32)
                if at < row_bits:
                    kept, sent = split(part, row, orders[k][at], n_col)
            return part

        def finish(parts):
            for bit in reversed(range(col_bits)):
                halves = [split(part, col, bit, 1) for part in parts]
                got = swap(jnp.concatenate([h[1] for h in halves]), "col", bit, n_col).astype(F32)
                parts, used = [], 0
                for kept, _ in halves:
                    parts.append(kept + got[used : used + kept.shape[0]])
                    used += kept.shape[0]
            part = jnp.concatenate(parts).astype(BF16)
            each = part.shape[0]
            for bit in reversed(orders[0]):
                got = swap(part, "row", bit, n_row)
                lower = ((row >> bit) & 1) == 0
                part = jnp.where(lower, jnp.concatenate([part, got]), jnp.concatenate([got, part]))
            out, used = [], 0
            for p in parts:
                out.append(part.reshape(n_row, each, unordered)[:, used : used + p.shape[0]])
                used += p.shape[0]
            return out

        def natural(blocks, k):
            shape = (2,) * row_bits
            axes = [orders[0].index(bit) for bit in orders[k]]
            moved = blocks.reshape(shape + blocks.shape[1:]).transpose(axes + [row_bits, row_bits + 1])
            return moved.reshape(-1, unordered)

        sums = [over_row(k, at, *pair) for k, (at, pair) in enumerate(state)]
        merged = finish(sums[:-1]) + finish(sums[-1:]) if len(sums) > 1 else finish(sums)
        whole = jnp.concatenate([natural(blocks, k) for k, blocks in enumerate(merged)])

        own = con_pairs.shape[0] // n_row
        return pl.pallas_call(
            functools.partial(pick_kernel, n_col, count, float(grid ** (-0.5))),
            in_specs=[smem] + [vmem] * 2,
            out_specs=vmem,
            out_shape=jax.ShapeDtypeStruct((own, per_col), F32),
            compiler_params=params(20),
            name="pick",
        )(place, con_pairs.T, whole)

    in_specs = (P("row", "col"), P(None, "col"), P(), P(), P())

    return jax.shard_map(per_device, mesh=mesh, in_specs=in_specs, out_specs=P("row", "col"), check_vma=False)
```

```python
import functools

import jax
import jax.numpy as jnp
from jax import lax
from jax.experimental import pallas as pl
from jax.experimental.pallas import tpu as pltpu
from jax.sharding import PartitionSpec as P


CHUNKS = 4

F32, BF16 = jnp.float32, jnp.bfloat16
CONTRACT_MINOR = (((1,), (1,)), ((), ()))


def one_hot_columns(index, count):
    numbers = lax.broadcasted_iota(jnp.int32, (count, index.shape[1]), 0)
    return jnp.where(numbers == index, 1.0, 0.0)


def groups(ref, n_col, start, width):
    each = ref.shape[0] // n_col
    return jnp.concatenate([ref[z * each + start : z * each + start + width, :] for z in range(n_col)])


def build_val(first, second, val_ref, val_density):
    grid = val_ref.shape[1]
    step = min(2048, grid)

    @pl.loop(0, grid // step)
    def _(i):
        at = pl.ds(pl.multiple_of(i * step, step), step)
        orbitals = val_ref[:, at]
        a = jnp.dot(first, orbitals, preferred_element_type=F32)
        b = jnp.dot(second, orbitals, preferred_element_type=F32)
        val_density[:, at] = (a * b).astype(BF16)


def build_con(con, rolled, density):
    count, columns = con.shape
    wide = min(512, columns)
    apart = density.shape[0] // count

    @pl.loop(0, columns // wide)
    def _(i):
        at = pl.ds(pl.multiple_of(i * wide, wide), wide)
        one = con[:, at].astype(F32)
        for shift in range(8):
            moved = one if shift == 0 else jnp.concatenate([one[shift:], one[:shift]])
            rolled[0:count, :] = moved
            rolled[count : 2 * count, :] = moved
            for d in range(shift, apart, 8):
                other = rolled[d - shift : d - shift + count, :]
                density[d * count : (d + 1) * count, at] = (one * other).astype(BF16)


def product(numbers, w, density, val_density):
    stripe = w[0].shape[0]
    t = [lax.dot_general(val_density[...], w[s][...], CONTRACT_MINOR, preferred_element_type=F32).astype(BF16) for s in numbers]
    rows = slice(numbers[0] * stripe, (numbers[-1] + 1) * stripe)
    return lax.dot_general(jnp.concatenate(t, axis=1), density[:, rows], CONTRACT_MINOR, preferred_element_type=F32)


def hand_out(n_col, mine, acc, kept, sent):
    half = kept[0].shape[0] // n_col
    for c, own in enumerate(kept):
        for z in range(n_col):
            first = (z * len(kept) + c) * 2
            to = slice(z * half, (z + 1) * half)
            own[to, :] = acc[pl.ds(pl.multiple_of((first + mine) * half, half), half), :]
            to = slice((c * n_col + z) * half, (c * n_col + z + 1) * half)
            sent[to, :] = acc[pl.ds(pl.multiple_of((first + 1 - mine) * half, half), half), :].astype(BF16)


def first_kernel(n_col, width, n_stripes, n_chunks, place, pairs, val, con_all, w_hbm, *refs):
    kept, sent, refs = refs[:n_chunks], refs[n_chunks], refs[n_chunks + 1 :]
    w, refs = refs[:n_stripes], refs[n_stripes:]
    density, hot1, hot2, val_density, acc, pairs_here, val_here, con, rolled, sems, in_sems = refs
    me = place[0] // n_col
    columns, stripe = con.shape[1], w[0].shape[0]
    fetches = [
        pltpu.make_async_copy(pairs, pairs_here, in_sems.at[0]),
        pltpu.make_async_copy(val, val_here, in_sems.at[1]),
        pltpu.make_async_copy(
            con_all.at[:, pl.ds(pl.multiple_of(me * columns, columns), columns)], con, in_sems.at[2]
        ),
    ]
    for fetch in fetches:
        fetch.start()
    copies = []
    for s in range(n_stripes):
        copies.append(pltpu.make_async_copy(w_hbm.at[pl.ds(s * stripe, stripe), :], w[s], sems.at[s]))
        copies[-1].start()
    fetches[0].wait()
    hot1[...] = one_hot_columns(pairs_here[0:1, :], hot1.shape[1]).T.astype(BF16)
    hot2[...] = one_hot_columns(pairs_here[1:2, :], hot2.shape[1]).T.astype(BF16)
    fetches[1].wait()
    build_val(groups(hot1, n_col, 0, width), groups(hot2, n_col, 0, width), val_here, val_density)
    fetches[2].wait()
    build_con(con, rolled, density)
    at_once = 2 - n_stripes % 2
    for s in range(0, n_stripes, at_once):
        for copy in copies[s : s + at_once]:
            copy.wait()
        part = product(list(range(s, s + at_once)), w, density, val_density)
        if s == 0:
            acc[...] = part
        else:
            acc[...] += part
    hand_out(n_col, me % 2, acc, kept, sent)


def begin_kernel(n_col, start, width, n_stripes, numbers, n_after, *refs):
    w, refs = refs[:n_stripes], refs[n_stripes:]
    (density, hot1, hot2, val), refs = refs[:4], refs[4:]
    acc, val_density, *_ = refs[n_after:]
    build_val(groups(hot1, n_col, start, width), groups(hot2, n_col, start, width), val, val_density)
    acc[...] = product(numbers, w, density, val_density)


def end_kernel(n_col, n_stripes, numbers, n_after, place, *refs):
    w, refs = refs[:n_stripes], refs[n_stripes:]
    (density, before, val_density), refs = refs[:3], refs[3:]
    kept, sent, acc = *refs[n_after : n_after + 2], refs[-1]
    acc[...] = before[...] + product(numbers, w, density, val_density)
    hand_out(n_col, place[0] // n_col % 2, acc, [kept], sent)


def fold_kernel(n_col, targets, got_groups, sent_groups, place, *refs):
    n = len(targets)
    kept, got = refs[:n], refs[n : n + len(got_groups)]
    out = refs[n + len(got_groups) :]
    halves, sent = out[: len(out) - len(sent_groups)], out[len(out) - len(sent_groups) :]
    source, sink = {}, {}
    for array, group in zip(got, got_groups):
        at = 0
        for c in group:
            source[c] = array, at
            at += kept[c].shape[0]
    for array, group in zip(sent, sent_groups):
        at = 0
        for c in group:
            sink[c] = array, at
            at += kept[c].shape[0] // (2 if targets[c] else 1)
    for c, target in enumerate(targets):
        part, rows = kept[c], kept[c].shape[0]
        (array, at), (other, to) = source[c], sink[c]
        if target is None:
            other[to : to + rows, :] = (part[...] + array[at : at + rows, :].astype(F32)).astype(BF16)
            continue
        axis, bit, each = target
        me = place[0] // n_col if axis == "row" else place[0] % n_col
        high = (me >> bit) % 2 == 1
        half = rows // each // 2
        for z in range(each):
            a, b = 2 * z * half, (2 * z + 1) * half
            low_part = part[a : a + half, :] + array[at + a : at + a + half, :].astype(F32)
            high_part = part[b : b + half, :] + array[at + b : at + b + half, :].astype(F32)
            halves[c][z * half : (z + 1) * half, :] = jnp.where(high, high_part, low_part)
            other[to + z * half : to + (z + 1) * half, :] = jnp.where(high, low_part, high_part).astype(BF16)


def pick_kernel(n_col, count, scale, gathers, place, pairs, *refs):
    arrays, (out, whole) = refs[: len(gathers)], refs[len(gathers) :]
    own = out.shape[0]
    me = place[0] // n_col
    for array, (steps, chunks) in zip(arrays, gathers):
        each = sum(rows for _, rows, _ in chunks)
        for j in range(array.shape[0] // each):
            block = sum((((me ^ j) >> bit) % 2) << s for s, bit in enumerate(steps))
            used = 0
            for start, rows, order in chunks:
                spot = sum(((j >> bit) & 1) << (len(order) - 1 - s) for s, bit in enumerate(order))
                to = start + spot * rows
                whole[to : to + rows, :] = array[pl.ds(block * each + used, rows), :]
                used += rows
    if own % 128:
        every = pairs[...]
        asked = functools.reduce(
            lambda a, i: jnp.where(me == i, every[:, i * own : (i + 1) * own], a), range(pairs.shape[1] // own), every[:, :own]
        )
    else:
        asked = pairs[:, pl.ds(pl.multiple_of(me * own, own), own)]
    c, other = asked[0:1], asked[1:2]
    apart = jnp.where(other >= c, other - c, other - c + count)
    row = jnp.where(apart <= count // 2, apart * count + c, (count - apart) * count + other)
    pick = one_hot_columns(row, whole.shape[1]).astype(BF16)
    out[...] = (jnp.dot(whole[...].astype(BF16), pick, preferred_element_type=F32) * scale).T


def swap(x, axis, bit, size):
    return lax.ppermute(x, axis, [(i, i ^ (1 << bit)) for i in range(size)])


def solution(mesh):
    n_row, n_col = mesh.shape["row"], mesh.shape["col"]
    row_bits, col_bits = n_row.bit_length() - 1, n_col.bit_length() - 1

    def per_device(screened, val_orbitals, con_orbitals, val_pairs, con_pairs):
        own_rows, own_columns = screened.shape
        count, grid = con_orbitals.shape
        n_val = val_orbitals.shape[0]
        blocks = count // 2 + 1
        while blocks * count % 128:
            blocks += 1
        unordered = blocks * count
        n_pairs = val_pairs.shape[0]
        per_col = n_pairs // n_col
        chunks = CHUNKS if n_pairs >= 8 * CHUNKS * n_row * n_col and row_bits > 2 else 1
        width = per_col // chunks
        starts = [k * width for k in range(chunks)]
        place = (lax.axis_index("row") * n_col + lax.axis_index("col")).astype(jnp.int32)[None]
        smem = pl.BlockSpec(memory_space=pltpu.SMEM)
        vmem = pl.BlockSpec(memory_space=pltpu.VMEM)
        anywhere = pl.BlockSpec(memory_space=pl.ANY)
        hbm = pl.BlockSpec(memory_space=pltpu.HBM)

        def params(mib):
            return pltpu.CompilerParams(vmem_limit_bytes=mib << 20)

        def cost(n, rows):
            return pl.CostEstimate(
                flops=2 * n * rows * (own_columns + unordered), bytes_accessed=1 << 20, transcendentals=0
            )

        def outs(rows):
            return [pltpu.VMEM((rows, unordered), F32), pltpu.VMEM((rows, unordered), BF16)]

        stripe = min(512, own_rows)
        hots = [pltpu.VMEM((n_pairs, n_val), BF16)] * 2
        n_first = min(chunks, 2)
        n = n_col * width * n_first
        n_stripes = own_rows // stripe
        held = [pltpu.VMEM((stripe, own_columns), BF16)] * n_stripes + [pltpu.VMEM((unordered, own_rows), BF16)]
        n_held = n_stripes + 1
        *kept, sent = [pltpu.VMEM((n // n_first // 2, unordered), F32)] * n_first + [pltpu.VMEM((n // 2, unordered), BF16)]
        out = pl.pallas_call(
            functools.partial(first_kernel, n_col, width * n_first, n_stripes, n_first),
            in_specs=[smem] + [hbm] * 4,
            out_specs=[vmem] * (n_first + 1 + n_held + 2),
            out_shape=kept + [sent] + held + hots,
            scratch_shapes=[
                pltpu.VMEM((n, own_columns), BF16),
                pltpu.VMEM((n, unordered), F32),
                pltpu.VMEM((2, n_pairs), jnp.int32),
                pltpu.VMEM((n_val, own_columns), BF16),
                pltpu.VMEM((count, own_rows), BF16),
                pltpu.VMEM((2 * count, min(512, own_rows)), F32),
                pltpu.SemaphoreType.DMA((n_stripes,)),
                pltpu.SemaphoreType.DMA((3,)),
            ],
            compiler_params=params(18),
            cost_estimate=cost(n, own_rows),
            name="first",
        )(place, *[pltpu.with_memory_space_constraint(x, pltpu.HBM) for x in (val_pairs.T, val_orbitals, con_orbitals, screened)])
        kept, sent, fixed = list(out[:n_first]), out[n_first], list(out[n_first + 1 :])

        def begin(k, numbers, fixed, after):
            n = n_col * width
            acc, val_density, *fixed = pl.pallas_call(
                functools.partial(begin_kernel, n_col, starts[k], width, n_stripes, numbers, len(after)),
                in_specs=[vmem] * (n_held + 3) + [anywhere] * len(after),
                out_specs=[vmem] * (2 + n_held + 2),
                out_shape=[pltpu.VMEM((n, unordered), F32), pltpu.VMEM((n, own_columns), BF16)] + held + hots,
                input_output_aliases={i: 2 + i for i in range(n_held + 2)},
                compiler_params=params(7),
                cost_estimate=cost(n, len(numbers) * stripe),
            )(*fixed, val_orbitals, *after)
            return (acc, val_density), fixed

        def end(numbers, fixed, before, after):
            n = n_col * width
            kept, sent, *same = pl.pallas_call(
                functools.partial(end_kernel, n_col, n_stripes, numbers, len(after)),
                in_specs=[smem] + [vmem] * (n_held + 2) + [anywhere] * len(after),
                out_specs=[vmem] * (2 + n_held),
                out_shape=outs(n // 2) + held,
                scratch_shapes=[pltpu.VMEM((n, unordered), F32)],
                input_output_aliases={1 + i: 2 + i for i in range(n_held)},
                compiler_params=params(9),
                cost_estimate=cost(n, len(numbers) * stripe),
            )(place, *fixed[:n_held], *before, *after)
            return (kept, sent), same + fixed[n_held:]

        def fold(kept, got, targets, got_groups=None, sent_groups=None):
            everything = [list(range(len(kept)))]
            got_groups, sent_groups = got_groups or everything, sent_groups or everything
            rows = [k.shape[0] // (2 if t else 1) for k, t in zip(kept, targets)]
            shapes = [pltpu.VMEM((r, unordered), F32) for r, t in zip(rows, targets) if t]
            n_kept = len(shapes)
            shapes += [pltpu.VMEM((sum(rows[c] for c in g), unordered), BF16) for g in sent_groups]
            out = pl.pallas_call(
                functools.partial(fold_kernel, n_col, targets, got_groups, sent_groups),
                in_specs=[smem] + [vmem] * (len(kept) + len(got)),
                out_specs=[vmem] * len(shapes),
                out_shape=shapes,
                compiler_params=params(4),
            )(place, *kept, *got)
            return list(out[:n_kept]), list(out[n_kept:])

        order = list(range(1, row_bits))
        orders = [[0] + (order if k % 2 == 0 else order[::-1]) for k in range(chunks)]
        steps = [
            [("row", bit, n_col) for bit in orders[k]] + [("col", bit, 1) for bit in reversed(range(col_bits))] + [None]
            for k in range(chunks)
        ]
        n_steps = row_bits + col_bits
        sizes = {"row": n_row, "col": n_col}

        def send(k, at, sent):
            axis, bit, _ = steps[k][at]
            return swap(sent, axis, bit, sizes[axis])

        def run(k, at, until, kept, sent):
            for s in range(at, until):
                got = send(k, s, sent)
                kept, (sent,) = fold(kept, [got], [steps[k][s + 1]] * len(kept))
            return kept, sent

        def gather(part, bits):
            for bit in bits:
                part = jnp.concatenate([part, swap(part, "row", bit, n_row)])
            return part.astype(F32)

        if chunks > 1:
            low, high = list(range(n_stripes // 2)), list(range(n_stripes // 2, n_stripes))
            apart = [[0], [1]]
            before, fixed = begin(2, low, fixed, [sent])
            got = [send(0, 0, sent)]
            kept, sents = fold(kept, got, [steps[0][1], steps[1][1]], None, apart)
            m, fixed = end(high, fixed, before, sents)
            got = [send(k, 1, sents[k]) for k in range(2)]
            before, fixed = begin(3, low, fixed, [m[1]])
            kept, sents = fold(kept, got, [steps[0][2], steps[1][2]], apart, apart)
            m = run(2, 0, 1, [m[0]], m[1])
            b, fixed = end(high, fixed, before, sents + [m[1]])
            b = [b[0]], b[1]
            for s in range(2, row_bits):
                got = [send(k, s, sents[k]) for k in range(2)]
                ends = apart if s < row_bits - 1 else None
                kept, sents = fold(kept, got, [steps[0][s + 1], steps[1][s + 1]], apart, ends)
            a, sent = run(0, row_bits, n_steps - 1, kept, sents[0])
            m, m_sent = run(2, 1, n_steps - 1, *m)
            got = [send(0, n_steps - 1, sent), send(2, n_steps - 1, m_sent)]
            _, (early,) = fold(a + m, got, [None] * 3, [[0, 1], [2]], None)
            _, late = run(3, 0, n_steps, *b)
            early_bits, late_bits = order + [0], order[::-1] + [0]
            arrays = [gather(early, early_bits), gather(late, late_bits)]
            gathers = [(early_bits, [0, 1, 2]), (late_bits, [3])]
        else:
            _, late = run(0, 0, n_steps, kept, sent)
            late_bits = order[::-1] + [0]
            arrays, gathers = [gather(late, late_bits)], [(late_bits, [0])]
        gathers = [(bits, [(starts[k], width // n_row, orders[k]) for k in ks]) for bits, ks in gathers]

        own = con_pairs.shape[0] // n_row
        return pl.pallas_call(
            functools.partial(pick_kernel, n_col, count, float(grid ** (-0.5)), gathers),
            in_specs=[smem] + [vmem] * (1 + len(arrays)),
            out_specs=vmem,
            out_shape=jax.ShapeDtypeStruct((own, per_col), F32),
            scratch_shapes=[pltpu.VMEM((per_col, unordered), F32)],
            compiler_params=params(20),
            name="pick",
        )(place, con_pairs.T, *arrays)

    in_specs = (P("row", "col"), P(None, "col"), P(), P(), P())

    return jax.shard_map(per_device, mesh=mesh, in_specs=in_specs, out_specs=P("row", "col"), check_vma=False)
```

```python
import functools

import jax
import jax.numpy as jnp
from jax import lax
from jax.experimental import pallas as pl
from jax.experimental.pallas import tpu as pltpu
from jax.sharding import PartitionSpec as P


CHUNKS = 4

F32, BF16 = jnp.float32, jnp.bfloat16
CONTRACT_MINOR = (((1,), (1,)), ((), ()))


def one_hot_columns(index, count):
    numbers = lax.broadcasted_iota(jnp.int32, (count, index.shape[1]), 0)
    return jnp.where(numbers == index, 1.0, 0.0)


def groups(ref, n_col, start, width):
    each = ref.shape[0] // n_col
    return jnp.concatenate([ref[z * each + start : z * each + start + width, :] for z in range(n_col)])


def build_val(first, second, val_ref, val_density):
    grid = val_ref.shape[1]
    step = min(2048, grid)

    @pl.loop(0, grid // step)
    def _(i):
        at = pl.ds(pl.multiple_of(i * step, step), step)
        orbitals = val_ref[:, at]
        a = jnp.dot(first, orbitals, preferred_element_type=F32)
        b = jnp.dot(second, orbitals, preferred_element_type=F32)
        val_density[:, at] = (a * b).astype(BF16)


def build_con(con, rolled, density):
    count, columns = con.shape
    wide = min(512, columns)
    apart = density.shape[0] // count

    @pl.loop(0, columns // wide)
    def _(i):
        at = pl.ds(pl.multiple_of(i * wide, wide), wide)
        one = con[:, at].astype(F32)
        for shift in range(8):
            moved = one if shift == 0 else jnp.concatenate([one[shift:], one[:shift]])
            rolled[0:count, :] = moved
            rolled[count : 2 * count, :] = moved
            for d in range(shift, apart, 8):
                other = rolled[d - shift : d - shift + count, :]
                density[d * count : (d + 1) * count, at] = (one * other).astype(BF16)


def product(numbers, w, density, val_density):
    stripe = w[0].shape[0]
    t = [lax.dot_general(val_density[...], w[s][...], CONTRACT_MINOR, preferred_element_type=F32).astype(BF16) for s in numbers]
    rows = slice(numbers[0] * stripe, (numbers[-1] + 1) * stripe)
    return lax.dot_general(jnp.concatenate(t, axis=1), density[:, rows], CONTRACT_MINOR, preferred_element_type=F32)


def hand_out(n_col, mine, acc, kept, sent):
    half = kept[0].shape[0] // n_col
    for c, own in enumerate(kept):
        for z in range(n_col):
            first = (z * len(kept) + c) * 2
            to = slice(z * half, (z + 1) * half)
            own[to, :] = acc[pl.ds(pl.multiple_of((first + mine) * half, half), half), :]
            to = slice((c * n_col + z) * half, (c * n_col + z + 1) * half)
            sent[to, :] = acc[pl.ds(pl.multiple_of((first + 1 - mine) * half, half), half), :].astype(BF16)


def fetch_all(n_col, n_stripes, place, hbm, vmem, sems, in_sems):
    pairs, val, con_all, w_hbm = hbm
    pairs_here, val_here, con, w = vmem
    columns, stripe = con.shape[1], w[0].shape[0]
    mine = pl.ds(pl.multiple_of((place[0] // n_col) * columns, columns), columns)
    fetches = [
        pltpu.make_async_copy(pairs, pairs_here, in_sems.at[0]),
        pltpu.make_async_copy(val, val_here, in_sems.at[1]),
        pltpu.make_async_copy(con_all.at[:, mine], con, in_sems.at[2]),
    ]
    fetches += [
        pltpu.make_async_copy(w_hbm.at[pl.ds(s * stripe, stripe), :], w[s], sems.at[s]) for s in range(n_stripes)
    ]
    for fetch in fetches:
        fetch.start()
    return fetches[:3], fetches[3:]


def make_hot(pairs, hot1, hot2):
    hot1[...] = one_hot_columns(pairs[0:1, :], hot1.shape[1]).T.astype(BF16)
    hot2[...] = one_hot_columns(pairs[1:2, :], hot2.shape[1]).T.astype(BF16)


def single_kernel(n_col, n_stripes, place, pairs, val, con_all, w_hbm, kept, sent, val_density, acc, density, hot1, hot2, pairs_here, val_here, con, rolled, sems, in_sems, *w):
    inputs, stripes = fetch_all(n_col, n_stripes, place, (pairs, val, con_all, w_hbm), (pairs_here, val_here, con, w), sems, in_sems)
    for fetch in inputs:
        fetch.wait()
    make_hot(pairs_here, hot1, hot2)
    build_val(hot1[...], hot2[...], val_here, val_density)
    build_con(con, rolled, density)
    for fetch in stripes:
        fetch.wait()
    acc[...] = product(list(range(n_stripes)), w, density, val_density)
    hand_out(n_col, place[0] // n_col % 2, acc, [kept], sent)


def load_kernel(n_col, start, width, n_stripes, place, pairs, val, con_all, w_hbm, kept, sent, val_a, *refs):
    w, refs = refs[:n_stripes], refs[n_stripes:]
    density, hot1, hot2, val_b, pairs_here, val_here, con, rolled, sems, in_sems = refs
    inputs, stripes = fetch_all(n_col, n_stripes, place, (pairs, val, con_all, w_hbm), (pairs_here, val_here, con, w), sems, in_sems)
    inputs[0].wait()
    make_hot(pairs_here, hot1, hot2)
    inputs[1].wait()
    build_val(groups(hot1, n_col, start, width), groups(hot2, n_col, start, width), val_here, val_b)
    build_val(groups(hot1, n_col, 0, 2 * width), groups(hot2, n_col, 0, 2 * width), val_here, val_a)
    inputs[2].wait()
    build_con(con, rolled, density)
    high = place[0] % n_col % 2 == 1
    for s, fetch in enumerate(stripes):
        fetch.wait()
        stripe = w[s].shape[0]
        at = slice(s * stripe, (s + 1) * stripe)
        t = lax.dot_general(val_b[...], w[s][...], CONTRACT_MINOR, preferred_element_type=F32)
        for z in range(n_col // 2):
            to = slice(z * width, (z + 1) * width)
            low_part = t[2 * z * width : (2 * z + 1) * width, :]
            high_part = t[(2 * z + 1) * width : (2 * z + 2) * width, :]
            kept[to, at] = jnp.where(high, high_part, low_part)
            sent[to, at] = jnp.where(high, low_part, high_part).astype(BF16)


def pair_kernel(n_col, n_stripes, n_after, place, *refs):
    w, refs = refs[:n_stripes], refs[n_stripes:]
    (density, val_density), refs = refs[:2], refs[2 + n_after :]
    kept, sent, acc = refs[:2], refs[2], refs[-1]
    at_once = 2 - n_stripes % 2
    for s in range(0, n_stripes, at_once):
        part = product(list(range(s, s + at_once)), w, density, val_density)
        if s == 0:
            acc[...] = part
        else:
            acc[...] += part
    hand_out(n_col, place[0] // n_col % 2, acc, kept, sent)


def last_kernel(n_col, n_after, place, density, t, *refs):
    kept, sent, acc = refs[n_after:]
    acc[...] = lax.dot_general(t[...], density[...], CONTRACT_MINOR, preferred_element_type=F32)
    hand_out(1, place[0] // n_col % 2, acc, [kept], sent)


def begin_kernel(n_col, start, width, n_stripes, numbers, n_after, *refs):
    w, refs = refs[:n_stripes], refs[n_stripes:]
    (density, hot1, hot2, val), refs = refs[:4], refs[4:]
    acc, val_density, *_ = refs[n_after:]
    build_val(groups(hot1, n_col, start, width), groups(hot2, n_col, start, width), val, val_density)
    acc[...] = product(numbers, w, density, val_density)


def end_kernel(n_col, n_stripes, numbers, n_after, place, *refs):
    w, refs = refs[:n_stripes], refs[n_stripes:]
    (density, before, val_density), refs = refs[:3], refs[3:]
    kept, sent, acc = *refs[n_after : n_after + 2], refs[-1]
    acc[...] = before[...] + product(numbers, w, density, val_density)
    hand_out(n_col, place[0] // n_col % 2, acc, [kept], sent)


def fold_kernel(n_col, targets, got_groups, sent_groups, place, *refs):
    n = len(targets)
    kept, got = refs[:n], refs[n : n + len(got_groups)]
    out = refs[n + len(got_groups) :]
    halves, sent = out[: len(out) - len(sent_groups)], out[len(out) - len(sent_groups) :]
    source, sink = {}, {}
    for array, group in zip(got, got_groups):
        at = 0
        for c in group:
            source.setdefault(c, []).append((array, at))
            at += kept[c].shape[0]
    for array, group in zip(sent, sent_groups):
        at = 0
        for c in group:
            sink[c] = array, at
            at += kept[c].shape[0] // (2 if targets[c] else 1)
    for c, target in enumerate(targets):
        rows, (other, to) = kept[c].shape[0], sink[c]

        def part(first, size, c=c):
            total = kept[c][first : first + size, :]
            for array, at in source[c]:
                total = total + array[at + first : at + first + size, :].astype(F32)
            return total

        if target is None:
            other[to : to + rows, :] = part(0, rows).astype(BF16)
            continue
        axis, bit, each = target
        me = place[0] // n_col if axis == "row" else place[0] % n_col
        high = (me >> bit) % 2 == 1
        half = rows // each // 2
        for z in range(each):
            a, b = 2 * z * half, (2 * z + 1) * half
            low_part, high_part = part(a, half), part(b, half)
            halves[c][z * half : (z + 1) * half, :] = jnp.where(high, high_part, low_part)
            other[to + z * half : to + (z + 1) * half, :] = jnp.where(high, low_part, high_part).astype(BF16)


def quarter_kernel(n_col, bits, place, kept, got, kept_out, *refs):
    *sent, part = refs
    part[...] = kept[...] + got[...].astype(F32)
    me = place[0] // n_col
    first, second = (me >> bits[0]) % 2, (me >> bits[1]) % 2
    size = kept_out.shape[0] // n_col
    for flip, out in enumerate([kept_out, *sent]):
        at = ((first + flip // 2) % 2 * 2 + (second + flip % 2) % 2) * size
        for z in range(n_col):
            rows = part[pl.ds(pl.multiple_of(z * 4 * size + at, size), size), :]
            out[z * size : (z + 1) * size, :] = rows.astype(out.dtype)


def hot_kernel(n_col, count, n_after, place, pairs, *refs):
    pick = refs[n_after]
    own = pick.shape[1]
    me = place[0] // n_col
    if own % 128:
        every = pairs[...]
        asked = functools.reduce(
            lambda a, i: jnp.where(me == i, every[:, i * own : (i + 1) * own], a), range(pairs.shape[1] // own), every[:, :own]
        )
    else:
        asked = pairs[:, pl.ds(pl.multiple_of(me * own, own), own)]
    c, other = asked[0:1], asked[1:2]
    apart = jnp.where(other >= c, other - c, other - c + count)
    row = jnp.where(apart <= count // 2, apart * count + c, (count - apart) * count + other)
    pick[...] = one_hot_columns(row, pick.shape[0]).astype(BF16)


def pick_kernel(n_col, scale, gathers, place, pick, *refs):
    arrays, (out, whole) = refs[: len(gathers)], refs[len(gathers) :]
    me = place[0] // n_col
    for array, (steps, chunks) in zip(arrays, gathers):
        each = sum(rows for _, rows, _ in chunks)
        for j in range(array.shape[0] // each):
            block = sum((((me ^ j) >> bit) % 2) << s for s, bit in enumerate(steps))
            used = 0
            for start, rows, order in chunks:
                spot = sum(((j >> bit) & 1) << (len(order) - 1 - s) for s, bit in enumerate(order))
                to = start + spot * rows
                whole[to : to + rows, :] = array[pl.ds(block * each + used, rows), :]
                used += rows
    out[...] = (jnp.dot(whole[...].astype(BF16), pick[...], preferred_element_type=F32) * scale).T


def swap(x, axis, bits, size):
    return lax.ppermute(x, axis, [(i, i ^ bits) for i in range(size)])


def solution(mesh):
    n_row, n_col = mesh.shape["row"], mesh.shape["col"]
    row_bits, col_bits = n_row.bit_length() - 1, n_col.bit_length() - 1

    def per_device(screened, val_orbitals, con_orbitals, val_pairs, con_pairs):
        own_rows, own_columns = screened.shape
        count, grid = con_orbitals.shape
        n_val = val_orbitals.shape[0]
        blocks = count // 2 + 1
        while blocks * count % 128:
            blocks += 1
        unordered = blocks * count
        n_pairs = val_pairs.shape[0]
        per_col = n_pairs // n_col
        chunks = CHUNKS if n_pairs >= 8 * CHUNKS * n_row * n_col and row_bits > 2 else 1
        width = per_col // chunks
        starts = [k * width for k in range(chunks)]
        place = (lax.axis_index("row") * n_col + lax.axis_index("col")).astype(jnp.int32)[None]
        smem = pl.BlockSpec(memory_space=pltpu.SMEM)
        vmem = pl.BlockSpec(memory_space=pltpu.VMEM)
        anywhere = pl.BlockSpec(memory_space=pl.ANY)
        hbm = pl.BlockSpec(memory_space=pltpu.HBM)

        def params(mib):
            return pltpu.CompilerParams(vmem_limit_bytes=mib << 20)

        def cost(n, rows):
            return pl.CostEstimate(
                flops=2 * n * rows * (own_columns + unordered), bytes_accessed=1 << 20, transcendentals=0
            )

        def outs(rows):
            return [pltpu.VMEM((rows, unordered), F32), pltpu.VMEM((rows, unordered), BF16)]

        stripe = min(512, own_rows)
        n_stripes = own_rows // stripe
        held = [pltpu.VMEM((stripe, own_columns), BF16)] * n_stripes + [pltpu.VMEM((unordered, own_rows), BF16)]
        hots = [pltpu.VMEM((n_pairs, n_val), BF16)] * 2
        n_held = n_stripes + 1
        arguments = (place, *[pltpu.with_memory_space_constraint(x, pltpu.HBM) for x in (val_pairs.T, val_orbitals, con_orbitals, screened)])
        inputs = [
            pltpu.VMEM((2, n_pairs), jnp.int32),
            pltpu.VMEM((n_val, own_columns), BF16),
            pltpu.VMEM((count, own_rows), BF16),
            pltpu.VMEM((2 * count, min(512, own_rows)), F32),
            pltpu.SemaphoreType.DMA((n_stripes,)),
            pltpu.SemaphoreType.DMA((3,)),
        ]
        n = n_col * width

        def single():
            return pl.pallas_call(
                functools.partial(single_kernel, n_col, n_stripes),
                in_specs=[smem] + [hbm] * 4,
                out_specs=[vmem] * 2,
                out_shape=outs(n // 2),
                scratch_shapes=[pltpu.VMEM((n, own_columns), BF16), pltpu.VMEM((n, unordered), F32), held[-1], *hots, *inputs, *held[:-1]],
                compiler_params=params(40),
                name="single",
            )(*arguments)

        def load():
            kept, sent, val_density, *fixed = pl.pallas_call(
                functools.partial(load_kernel, n_col, starts[3], width, n_stripes),
                in_specs=[smem] + [hbm] * 4,
                out_specs=[vmem] * (3 + n_held + 2),
                out_shape=[
                    pltpu.VMEM((n // 2, own_rows), F32),
                    pltpu.VMEM((n // 2, own_rows), BF16),
                    pltpu.VMEM((2 * n, own_columns), BF16),
                    *held,
                    *hots,
                ],
                scratch_shapes=[pltpu.VMEM((n, own_columns), BF16), *inputs],
                compiler_params=params(10),
                cost_estimate=cost(n, own_rows),
                name="load",
            )(*arguments)
            return kept, sent, val_density, fixed

        def pair(fixed, val_density, after):
            *out, sent = pl.pallas_call(
                functools.partial(pair_kernel, n_col, n_stripes, len(after)),
                in_specs=[smem] + [vmem] * (n_held + 1) + [anywhere] * len(after),
                out_specs=[vmem] * (3 + n_held),
                out_shape=[outs(n // 2)[0]] * 2 + [outs(n)[1]] + held,
                scratch_shapes=[pltpu.VMEM((2 * n, unordered), F32)],
                input_output_aliases={1 + i: 3 + i for i in range(n_held)},
                compiler_params=params(12),
                cost_estimate=cost(2 * n, own_rows),
                name="pair",
            )(place, *fixed[:n_held], val_density, *after), None
            out = out[0]
            return list(out[:2]), out[2], list(out[3:]) + fixed[n_held:]

        def last(density, t, after):
            rows = t.shape[0]
            return pl.pallas_call(
                functools.partial(last_kernel, n_col, len(after)),
                in_specs=[smem] + [vmem] * 2 + [anywhere] * len(after),
                out_specs=[vmem] * 2,
                out_shape=outs(rows // 2),
                scratch_shapes=[pltpu.VMEM((rows, unordered), F32)],
                compiler_params=params(8),
                cost_estimate=cost(rows, own_rows),
                name="last",
            )(place, density, t, *after)

        def begin(k, numbers, fixed, after):
            n = n_col * width
            acc, val_density, *fixed = pl.pallas_call(
                functools.partial(begin_kernel, n_col, starts[k], width, n_stripes, numbers, len(after)),
                in_specs=[vmem] * (n_held + 3) + [anywhere] * len(after),
                out_specs=[vmem] * (2 + n_held),
                out_shape=[pltpu.VMEM((n, unordered), F32), pltpu.VMEM((n, own_columns), BF16)] + held,
                input_output_aliases={i: 2 + i for i in range(n_held)},
                compiler_params=params(7),
                cost_estimate=cost(n, len(numbers) * stripe),
            )(*fixed, val_orbitals, *after)
            return (acc, val_density), fixed

        def end(numbers, fixed, before, after):
            n = n_col * width
            kept, sent, *same = pl.pallas_call(
                functools.partial(end_kernel, n_col, n_stripes, numbers, len(after)),
                in_specs=[smem] + [vmem] * (n_held + 2) + [anywhere] * len(after),
                out_specs=[vmem] * 3,
                out_shape=outs(n // 2) + held[-1:],
                scratch_shapes=[pltpu.VMEM((n, unordered), F32)],
                input_output_aliases={n_held: 2},
                compiler_params=params(7),
                cost_estimate=cost(n, len(numbers) * stripe),
            )(place, *fixed[:n_held], *before, *after)
            return (kept, sent), same[0]

        def fold(kept, got, targets, got_groups=None, sent_groups=None):
            everything = [list(range(len(kept)))]
            got_groups, sent_groups = got_groups or everything, sent_groups or everything
            rows = [k.shape[0] // (2 if t else 1) for k, t in zip(kept, targets)]
            minor = kept[0].shape[1]
            shapes = [pltpu.VMEM((r, minor), F32) for r, t in zip(rows, targets) if t]
            n_kept = len(shapes)
            shapes += [pltpu.VMEM((sum(rows[c] for c in g), minor), BF16) for g in sent_groups]
            out = pl.pallas_call(
                functools.partial(fold_kernel, n_col, targets, got_groups, sent_groups),
                in_specs=[smem] + [vmem] * (len(kept) + len(got)),
                out_specs=[vmem] * len(shapes),
                out_shape=shapes,
                compiler_params=params(4),
            )(place, *kept, *got)
            return list(out[:n_kept]), list(out[n_kept:])

        def quarters(kept, got, bits):
            rows = kept.shape[0] // 4
            kept, *sent = pl.pallas_call(
                functools.partial(quarter_kernel, n_col, bits),
                in_specs=[smem] + [vmem] * 2,
                out_specs=[vmem] * 4,
                out_shape=[pltpu.VMEM((rows, unordered), F32)] + [pltpu.VMEM((rows, unordered), BF16)] * 3,
                scratch_shapes=[pltpu.VMEM(kept.shape, F32)],
                compiler_params=params(4),
            )(place, kept, got)
            return kept, sent

        order = list(range(1, row_bits))
        orders = [[0] + (order if k % 2 == 0 else order[::-1]) for k in range(chunks)]
        col_steps = [("col", bit, n_col >> (bit + 1)) for bit in range(col_bits)]
        steps = [
            [("row", bit, n_col) for bit in orders[k]] + col_steps + [None] if k < 3
            else col_steps + [None] + [("row", bit, 1) for bit in orders[k]] + [None]
            for k in range(chunks)
        ]
        n_steps = row_bits + col_bits
        sizes = {"row": n_row, "col": n_col}

        def send(k, at, sent):
            axis, bit, _ = steps[k][at]
            return swap(sent, axis, 1 << bit, sizes[axis])

        def run(k, at, until, kept, sent):
            for s in range(at, until):
                got = send(k, s, sent)
                kept, (sent,) = fold(kept, [got], [steps[k][s + 1]] * len(kept))
            return kept, sent

        def gather(part, bits):
            for bit in bits:
                part = jnp.concatenate([part, swap(part, "row", 1 << bit, n_row)])
            return part.astype(F32)

        if chunks > 1:
            low, high = list(range(n_stripes // 2)), list(range(n_stripes // 2, n_stripes))
            apart = [[0], [1]]
            kept, b_sent, val_density, fixed = load()
            b = [kept], b_sent
            kept, sent, fixed = pair(fixed, val_density, [b_sent])
            b = run(3, 0, 1, *b)
            got = [send(0, 0, sent)]
            kept, sents = fold(kept, got, [steps[0][1], steps[1][1]], None, apart)
            before, fixed = begin(2, low, fixed, [b[1], *sents])
            m, density = end(high, fixed, before, [])
            m_kept, m_sent = quarters(m[0], send(2, 0, m[1]), orders[2][1:3])
            for s in range(1, row_bits):
                got = [send(k, s, sents[k]) for k in range(2)]
                ends = apart if s < row_bits - 1 else None
                kept, sents = fold(kept, got, [steps[0][s + 1], steps[1][s + 1]], apart, ends)
                if s == 1:
                    hold = sents
            b = run(3, 1, col_bits, *b)
            b_kept, b_sent = last(density, b[1], hold + m_sent)
            b = [b_kept], b_sent
            when = [b_sent]
            axis_steps = len(steps[3]) - 1
            for s in range(col_bits + 1, axis_steps):
                axis, bit, _ = steps[3][s]
                got = swap(b[1], axis, 1 << bit, sizes[axis])
                kept_b, (sent_b,) = fold(b[0], [got], [steps[3][s + 1]])
                b = kept_b, sent_b
            _, a_sums = run(0, row_bits, n_steps, kept, sents[0])
            flips = [1 << orders[2][2], 1 << orders[2][1], 1 << orders[2][1] | 1 << orders[2][2]]
            got = [swap(x, "row", flip, n_row) for x, flip in zip(m_sent, flips)]
            m_kept, m_sent = fold([m_kept], got, [steps[2][3]], [[0]] * 3)
            _, m_sums = run(2, 3, n_steps, m_kept, m_sent[0])
            up, down = order + [0], order[::-1] + [0]
            arrays = [gather(a_sums, down), gather(b[1], up), gather(m_sums, up)]
            gathers = [(down, [0, 1]), (up, [3]), (up, [2])]
        else:
            kept, sent = single()
            when = []
            _, late = run(0, 0, n_steps, [kept], sent)
            late_bits = order[::-1] + [0]
            arrays, gathers = [gather(late, late_bits)], [(late_bits, [0])]
        gathers = [(bits, [(starts[k], width // n_row, orders[k]) for k in ks]) for bits, ks in gathers]

        own = con_pairs.shape[0] // n_row
        pick = pl.pallas_call(
            functools.partial(hot_kernel, n_col, count, len(when)),
            in_specs=[smem, vmem] + [anywhere] * len(when),
            out_specs=vmem,
            out_shape=pltpu.VMEM((unordered, own), BF16),
            compiler_params=params(8),
            name="hot",
        )(place, con_pairs.T, *when)
        return pl.pallas_call(
            functools.partial(pick_kernel, n_col, float(grid ** (-0.5)), gathers),
            in_specs=[smem] + [vmem] * (1 + len(arrays)),
            out_specs=vmem,
            out_shape=jax.ShapeDtypeStruct((own, per_col), F32),
            scratch_shapes=[pltpu.VMEM((per_col, unordered), F32)],
            compiler_params=params(20),
            name="pick",
        )(place, pick, *arrays)

    in_specs = (P("row", "col"), P(None, "col"), P(), P(), P())

    return jax.shard_map(per_device, mesh=mesh, in_specs=in_specs, out_specs=P("row", "col"), check_vma=False)
```

```python
import functools

import jax
import jax.numpy as jnp
from jax import lax
from jax.experimental import pallas as pl
from jax.experimental.pallas import tpu as pltpu
from jax.sharding import PartitionSpec as P


CHUNKS = 4

F32, BF16 = jnp.float32, jnp.bfloat16
CONTRACT_MINOR = (((1,), (1,)), ((), ()))


def one_hot_columns(index, count):
    numbers = lax.broadcasted_iota(jnp.int32, (count, index.shape[1]), 0)
    return jnp.where(numbers == index, 1.0, 0.0)


def groups(ref, n_col, start, width):
    each = ref.shape[0] // n_col
    return jnp.concatenate([ref[z * each + start : z * each + start + width, :] for z in range(n_col)])


def build_val(first, second, val_ref, val_density):
    grid = val_ref.shape[1]
    step = min(2048, grid)

    @pl.loop(0, grid // step)
    def _(i):
        at = pl.ds(pl.multiple_of(i * step, step), step)
        orbitals = val_ref[:, at]
        a = jnp.dot(first, orbitals, preferred_element_type=F32)
        b = jnp.dot(second, orbitals, preferred_element_type=F32)
        val_density[:, at] = (a * b).astype(BF16)


def build_con(con, rolled, density):
    count, columns = con.shape
    wide = min(512, columns)
    apart = density.shape[0] // count

    @pl.loop(0, columns // wide)
    def _(i):
        at = pl.ds(pl.multiple_of(i * wide, wide), wide)
        one = con[:, at].astype(F32)
        for shift in range(8):
            moved = one if shift == 0 else jnp.concatenate([one[shift:], one[:shift]])
            rolled[0:count, :] = moved
            rolled[count : 2 * count, :] = moved
            for d in range(shift, apart, 8):
                other = rolled[d - shift : d - shift + count, :]
                density[d * count : (d + 1) * count, at] = (one * other).astype(BF16)


def product(numbers, w, density, val_density):
    stripe = w[0].shape[0]
    t = [lax.dot_general(val_density[...], w[s][...], CONTRACT_MINOR, preferred_element_type=F32).astype(BF16) for s in numbers]
    rows = slice(numbers[0] * stripe, (numbers[-1] + 1) * stripe)
    return lax.dot_general(jnp.concatenate(t, axis=1), density[:, rows], CONTRACT_MINOR, preferred_element_type=F32)


def hand_out(n_col, mine, acc, kept, sent):
    half = kept[0].shape[0] // n_col
    for c, own in enumerate(kept):
        for z in range(n_col):
            first = (z * len(kept) + c) * 2
            to = slice(z * half, (z + 1) * half)
            own[to, :] = acc[pl.ds(pl.multiple_of((first + mine) * half, half), half), :]
            to = slice((c * n_col + z) * half, (c * n_col + z + 1) * half)
            sent[to, :] = acc[pl.ds(pl.multiple_of((first + 1 - mine) * half, half), half), :].astype(BF16)


def fetch_all(n_col, n_stripes, place, hbm, vmem, sems, in_sems):
    pairs, val, con_all, w_hbm = hbm
    pairs_here, val_here, con, w = vmem
    columns, stripe = con.shape[1], w[0].shape[0]
    mine = pl.ds(pl.multiple_of((place[0] // n_col) * columns, columns), columns)
    fetches = [
        pltpu.make_async_copy(pairs, pairs_here, in_sems.at[0]),
        pltpu.make_async_copy(val, val_here, in_sems.at[1]),
        pltpu.make_async_copy(con_all.at[:, mine], con, in_sems.at[2]),
    ]
    fetches += [
        pltpu.make_async_copy(w_hbm.at[pl.ds(s * stripe, stripe), :], w[s], sems.at[s]) for s in range(n_stripes)
    ]
    for fetch in fetches[:3]:
        fetch.start()
    return fetches[:3], fetches[3:]


def make_hot(pairs, hot1, hot2):
    hot1[...] = one_hot_columns(pairs[0:1, :], hot1.shape[1]).T.astype(BF16)
    hot2[...] = one_hot_columns(pairs[1:2, :], hot2.shape[1]).T.astype(BF16)


def single_kernel(n_col, n_stripes, place, pairs, val, con_all, w_hbm, kept, sent, val_density, acc, density, hot1, hot2, pairs_here, val_here, con, rolled, sems, in_sems, *w):
    inputs, stripes = fetch_all(n_col, n_stripes, place, (pairs, val, con_all, w_hbm), (pairs_here, val_here, con, w), sems, in_sems)
    for fetch in stripes:
        fetch.start()
    for fetch in inputs:
        fetch.wait()
    make_hot(pairs_here, hot1, hot2)
    build_val(hot1[...], hot2[...], val_here, val_density)
    build_con(con, rolled, density)
    for fetch in stripes:
        fetch.wait()
    acc[...] = product(list(range(n_stripes)), w, density, val_density)
    hand_out(n_col, place[0] // n_col % 2, acc, [kept], sent)


def load_kernel(n_col, start, width, n_stripes, place, pairs, val, con_all, w_hbm, kept, sent, val_a, *refs):
    w, refs = refs[:n_stripes], refs[n_stripes:]
    density, hot1, hot2, val_b, pairs_here, val_here, con, rolled, sems, in_sems = refs
    inputs, stripes = fetch_all(n_col, n_stripes, place, (pairs, val, con_all, w_hbm), (pairs_here, val_here, con, w), sems, in_sems)
    inputs[0].wait()
    inputs[1].wait()
    for fetch in stripes:
        fetch.start()
    make_hot(pairs_here, hot1, hot2)
    build_val(groups(hot1, n_col, start, width), groups(hot2, n_col, start, width), val_here, val_b)
    build_val(groups(hot1, n_col, 0, 2 * width), groups(hot2, n_col, 0, 2 * width), val_here, val_a)
    inputs[2].wait()
    build_con(con, rolled, density)
    high = place[0] % n_col % 2 == 1
    for s, fetch in enumerate(stripes):
        fetch.wait()
        stripe = w[s].shape[0]
        at = slice(s * stripe, (s + 1) * stripe)
        t = lax.dot_general(val_b[...], w[s][...], CONTRACT_MINOR, preferred_element_type=F32)
        for z in range(n_col // 2):
            to = slice(z * width, (z + 1) * width)
            low_part = t[2 * z * width : (2 * z + 1) * width, :]
            high_part = t[(2 * z + 1) * width : (2 * z + 2) * width, :]
            kept[to, at] = jnp.where(high, high_part, low_part)
            sent[to, at] = jnp.where(high, low_part, high_part).astype(BF16)


def pair_kernel(n_col, n_stripes, n_after, place, *refs):
    w, refs = refs[:n_stripes], refs[n_stripes:]
    (density, val_density), refs = refs[:2], refs[2 + n_after :]
    kept, sent, acc = refs[:2], refs[2], refs[-1]
    at_once = 2 - n_stripes % 2
    for s in range(0, n_stripes, at_once):
        part = product(list(range(s, s + at_once)), w, density, val_density)
        if s == 0:
            acc[...] = part
        else:
            acc[...] += part
    hand_out(n_col, place[0] // n_col % 2, acc, kept, sent)


def last_kernel(n_col, n_after, place, density, t, *refs):
    kept, sent, acc = refs[n_after:]
    acc[...] = lax.dot_general(t[...], density[...], CONTRACT_MINOR, preferred_element_type=F32)
    hand_out(1, place[0] // n_col % 2, acc, [kept], sent)


def begin_kernel(n_col, start, width, n_stripes, numbers, n_after, *refs):
    w, refs = refs[:n_stripes], refs[n_stripes:]
    (density, hot1, hot2, val), refs = refs[:4], refs[4:]
    acc, val_density, *_ = refs[n_after:]
    build_val(groups(hot1, n_col, start, width), groups(hot2, n_col, start, width), val, val_density)
    acc[...] = product(numbers, w, density, val_density)


def end_kernel(n_col, n_stripes, numbers, n_after, place, *refs):
    w, refs = refs[:n_stripes], refs[n_stripes:]
    (density, before, val_density), refs = refs[:3], refs[3:]
    kept, sent, acc = *refs[n_after : n_after + 2], refs[-1]
    acc[...] = before[...] + product(numbers, w, density, val_density)
    hand_out(n_col, place[0] // n_col % 2, acc, [kept], sent)


def fold_kernel(n_col, targets, got_groups, sent_groups, place, *refs):
    n = len(targets)
    kept, got = refs[:n], refs[n : n + len(got_groups)]
    out = refs[n + len(got_groups) :]
    halves, sent = out[: len(out) - len(sent_groups)], out[len(out) - len(sent_groups) :]
    source, sink = {}, {}
    for array, group in zip(got, got_groups):
        at = 0
        for c in group:
            source.setdefault(c, []).append((array, at))
            at += kept[c].shape[0]
    for array, group in zip(sent, sent_groups):
        at = 0
        for c in group:
            sink[c] = array, at
            at += kept[c].shape[0] // (2 if targets[c] else 1)
    for c, target in enumerate(targets):
        rows, (other, to) = kept[c].shape[0], sink[c]

        def part(first, size, c=c):
            total = kept[c][first : first + size, :]
            for array, at in source[c]:
                total = total + array[at + first : at + first + size, :].astype(F32)
            return total

        if target is None:
            other[to : to + rows, :] = part(0, rows).astype(BF16)
            continue
        axis, bit, each = target
        me = place[0] // n_col if axis == "row" else place[0] % n_col
        high = (me >> bit) % 2 == 1
        half = rows // each // 2
        for z in range(each):
            a, b = 2 * z * half, (2 * z + 1) * half
            low_part, high_part = part(a, half), part(b, half)
            halves[c][z * half : (z + 1) * half, :] = jnp.where(high, high_part, low_part)
            other[to + z * half : to + (z + 1) * half, :] = jnp.where(high, low_part, high_part).astype(BF16)


def quarter_kernel(n_col, bits, n_chunks, place, *refs):
    kept, got, refs = refs[:n_chunks], refs[n_chunks], refs[n_chunks + 1 :]
    kept_out, (*sent, part) = refs[:n_chunks], refs[n_chunks:]
    me = place[0] // n_col
    first, second = (me >> bits[0]) % 2, (me >> bits[1]) % 2
    rows = kept[0].shape[0]
    size = rows // 4 // n_col
    for c in range(n_chunks):
        part[...] = kept[c][...] + got[c * rows : (c + 1) * rows, :].astype(F32)
        for flip, out in enumerate([kept_out[c], *sent]):
            at = ((first + flip // 2) % 2 * 2 + (second + flip % 2) % 2) * size
            base = c * n_col * size if flip else 0
            for z in range(n_col):
                mine = part[pl.ds(pl.multiple_of(z * 4 * size + at, size), size), :]
                out[base + z * size : base + (z + 1) * size, :] = mine.astype(out.dtype)


def hot_kernel(n_col, count, n_after, place, pairs, *refs):
    pick = refs[n_after]
    own = pick.shape[1]
    me = place[0] // n_col
    if own % 128:
        every = pairs[...]
        asked = functools.reduce(
            lambda a, i: jnp.where(me == i, every[:, i * own : (i + 1) * own], a), range(pairs.shape[1] // own), every[:, :own]
        )
    else:
        asked = pairs[:, pl.ds(pl.multiple_of(me * own, own), own)]
    c, other = asked[0:1], asked[1:2]
    apart = jnp.where(other >= c, other - c, other - c + count)
    row = jnp.where(apart <= count // 2, apart * count + c, (count - apart) * count + other)
    pick[...] = one_hot_columns(row, pick.shape[0]).astype(BF16)


def pick_kernel(n_col, scale, gathers, place, pick, *refs):
    arrays, (out, whole) = refs[: len(gathers)], refs[len(gathers) :]
    me = place[0] // n_col
    for array, (steps, chunks) in zip(arrays, gathers):
        each = sum(rows for _, rows, _ in chunks)
        for j in range(array.shape[0] // each):
            block = sum((((me ^ j) >> bit) % 2) << s for s, bit in enumerate(steps))
            used = 0
            for start, rows, order in chunks:
                spot = sum(((j >> bit) & 1) << (len(order) - 1 - s) for s, bit in enumerate(order))
                to = start + spot * rows
                whole[to : to + rows, :] = array[pl.ds(block * each + used, rows), :]
                used += rows
    out[...] = (jnp.dot(whole[...].astype(BF16), pick[...], preferred_element_type=F32) * scale).T


def swap(x, axis, bits, size):
    return lax.ppermute(x, axis, [(i, i ^ bits) for i in range(size)])


def solution(mesh):
    n_row, n_col = mesh.shape["row"], mesh.shape["col"]
    row_bits, col_bits = n_row.bit_length() - 1, n_col.bit_length() - 1

    def per_device(screened, val_orbitals, con_orbitals, val_pairs, con_pairs):
        own_rows, own_columns = screened.shape
        count, grid = con_orbitals.shape
        n_val = val_orbitals.shape[0]
        blocks = count // 2 + 1
        while blocks * count % 128:
            blocks += 1
        unordered = blocks * count
        n_pairs = val_pairs.shape[0]
        per_col = n_pairs // n_col
        chunks = CHUNKS if n_pairs >= 8 * CHUNKS * n_row * n_col and row_bits == 3 else 1
        width = per_col // chunks
        starts = [k * width for k in range(chunks)]
        place = (lax.axis_index("row") * n_col + lax.axis_index("col")).astype(jnp.int32)[None]
        smem = pl.BlockSpec(memory_space=pltpu.SMEM)
        vmem = pl.BlockSpec(memory_space=pltpu.VMEM)
        anywhere = pl.BlockSpec(memory_space=pl.ANY)
        hbm = pl.BlockSpec(memory_space=pltpu.HBM)

        def params(mib):
            return pltpu.CompilerParams(vmem_limit_bytes=mib << 20)

        def cost(n, rows):
            return pl.CostEstimate(
                flops=2 * n * rows * (own_columns + unordered), bytes_accessed=1 << 20, transcendentals=0
            )

        def outs(rows):
            return [pltpu.VMEM((rows, unordered), F32), pltpu.VMEM((rows, unordered), BF16)]

        stripe = min(512, own_rows)
        n_stripes = own_rows // stripe
        held = [pltpu.VMEM((stripe, own_columns), BF16)] * n_stripes + [pltpu.VMEM((unordered, own_rows), BF16)]
        hots = [pltpu.VMEM((n_pairs, n_val), BF16)] * 2
        n_held = n_stripes + 1
        arguments = (place, *[pltpu.with_memory_space_constraint(x, pltpu.HBM) for x in (val_pairs.T, val_orbitals, con_orbitals, screened)])
        inputs = [
            pltpu.VMEM((2, n_pairs), jnp.int32),
            pltpu.VMEM((n_val, own_columns), BF16),
            pltpu.VMEM((count, own_rows), BF16),
            pltpu.VMEM((2 * count, min(512, own_rows)), F32),
            pltpu.SemaphoreType.DMA((n_stripes,)),
            pltpu.SemaphoreType.DMA((3,)),
        ]
        n = n_col * width

        def single():
            return pl.pallas_call(
                functools.partial(single_kernel, n_col, n_stripes),
                in_specs=[smem] + [hbm] * 4,
                out_specs=[vmem] * 2,
                out_shape=outs(n // 2),
                scratch_shapes=[pltpu.VMEM((n, own_columns), BF16), pltpu.VMEM((n, unordered), F32), held[-1], *hots, *inputs, *held[:-1]],
                compiler_params=params(40),
                name="single",
            )(*arguments)

        def load():
            kept, sent, val_density, *fixed = pl.pallas_call(
                functools.partial(load_kernel, n_col, starts[3], width, n_stripes),
                in_specs=[smem] + [hbm] * 4,
                out_specs=[vmem] * (3 + n_held + 2),
                out_shape=[
                    pltpu.VMEM((n // 2, own_rows), F32),
                    pltpu.VMEM((n // 2, own_rows), BF16),
                    pltpu.VMEM((2 * n, own_columns), BF16),
                    *held,
                    *hots,
                ],
                scratch_shapes=[pltpu.VMEM((n, own_columns), BF16), *inputs],
                compiler_params=params(10),
                cost_estimate=cost(n, own_rows),
                name="load",
            )(*arguments)
            return kept, sent, val_density, fixed

        def pair(fixed, val_density, after):
            *out, sent = pl.pallas_call(
                functools.partial(pair_kernel, n_col, n_stripes, len(after)),
                in_specs=[smem] + [vmem] * (n_held + 1) + [anywhere] * len(after),
                out_specs=[vmem] * (3 + n_held),
                out_shape=[outs(n // 2)[0]] * 2 + [outs(n)[1]] + held,
                scratch_shapes=[pltpu.VMEM((2 * n, unordered), F32)],
                input_output_aliases={1 + i: 3 + i for i in range(n_held)},
                compiler_params=params(12),
                cost_estimate=cost(2 * n, own_rows),
                name="pair",
            )(place, *fixed[:n_held], val_density, *after), None
            out = out[0]
            return list(out[:2]), out[2], list(out[3:]) + fixed[n_held:]

        def last(density, t, after):
            rows = t.shape[0]
            return pl.pallas_call(
                functools.partial(last_kernel, n_col, len(after)),
                in_specs=[smem] + [vmem] * 2 + [anywhere] * len(after),
                out_specs=[vmem] * 2,
                out_shape=outs(rows // 2),
                scratch_shapes=[pltpu.VMEM((rows, unordered), F32)],
                compiler_params=params(8),
                cost_estimate=cost(rows, own_rows),
                name="last",
            )(place, density, t, *after)

        def begin(k, numbers, fixed, after):
            n = n_col * width
            acc, val_density, *fixed = pl.pallas_call(
                functools.partial(begin_kernel, n_col, starts[k], width, n_stripes, numbers, len(after)),
                in_specs=[vmem] * (n_held + 3) + [anywhere] * len(after),
                out_specs=[vmem] * (2 + n_held),
                out_shape=[pltpu.VMEM((n, unordered), F32), pltpu.VMEM((n, own_columns), BF16)] + held,
                input_output_aliases={i: 2 + i for i in range(n_held)},
                compiler_params=params(7),
                cost_estimate=cost(n, len(numbers) * stripe),
            )(*fixed, val_orbitals, *after)
            return (acc, val_density), fixed

        def end(numbers, fixed, before, after):
            n = n_col * width
            kept, sent, *same = pl.pallas_call(
                functools.partial(end_kernel, n_col, n_stripes, numbers, len(after)),
                in_specs=[smem] + [vmem] * (n_held + 2) + [anywhere] * len(after),
                out_specs=[vmem] * 3,
                out_shape=outs(n // 2) + held[-1:],
                scratch_shapes=[pltpu.VMEM((n, unordered), F32)],
                input_output_aliases={n_held: 2},
                compiler_params=params(7),
                cost_estimate=cost(n, len(numbers) * stripe),
            )(place, *fixed[:n_held], *before, *after)
            return (kept, sent), same[0]

        def fold(kept, got, targets, got_groups=None, sent_groups=None):
            everything = [list(range(len(kept)))]
            got_groups, sent_groups = got_groups or everything, sent_groups or everything
            rows = [k.shape[0] // (2 if t else 1) for k, t in zip(kept, targets)]
            minor = kept[0].shape[1]
            shapes = [pltpu.VMEM((r, minor), F32) for r, t in zip(rows, targets) if t]
            n_kept = len(shapes)
            shapes += [pltpu.VMEM((sum(rows[c] for c in g), minor), BF16) for g in sent_groups]
            out = pl.pallas_call(
                functools.partial(fold_kernel, n_col, targets, got_groups, sent_groups),
                in_specs=[smem] + [vmem] * (len(kept) + len(got)),
                out_specs=[vmem] * len(shapes),
                out_shape=shapes,
                compiler_params=params(4),
            )(place, *kept, *got)
            return list(out[:n_kept]), list(out[n_kept:])

        def quarters(kept, got, bits):
            rows = kept[0].shape[0] // 4
            out = pl.pallas_call(
                functools.partial(quarter_kernel, n_col, bits, len(kept)),
                in_specs=[smem] + [vmem] * (len(kept) + 1),
                out_specs=[vmem] * (len(kept) + 3),
                out_shape=[pltpu.VMEM((rows, unordered), F32)] * len(kept)
                + [pltpu.VMEM((rows * len(kept), unordered), BF16)] * 3,
                scratch_shapes=[pltpu.VMEM(kept[0].shape, F32)],
                compiler_params=params(6),
            )(place, *kept, got)
            sent = list(out[len(kept) :])
            flips = [1 << bits[1], 1 << bits[0], 1 << bits[0] | 1 << bits[1]]
            got = [swap(x, "row", flip, n_row) for x, flip in zip(sent, flips)]
            return list(out[: len(kept)]), got, sent

        order = list(range(1, row_bits))
        orders = [[0] + order for _ in range(chunks)]
        col_steps = [("col", bit, n_col >> (bit + 1)) for bit in range(col_bits)]
        steps = [
            [("row", bit, n_col) for bit in orders[k]] + col_steps + [None] if k < 3
            else col_steps + [None] + [("row", bit, 1) for bit in orders[k]] + [None]
            for k in range(chunks)
        ]
        n_steps = row_bits + col_bits
        sizes = {"row": n_row, "col": n_col}

        def send(k, at, sent):
            axis, bit, _ = steps[k][at]
            return swap(sent, axis, 1 << bit, sizes[axis])

        def run(k, at, until, kept, sent):
            for s in range(at, until):
                got = send(k, s, sent)
                kept, (sent,) = fold(kept, [got], [steps[k][s + 1]] * len(kept))
            return kept, sent

        def gather(part, bits):
            for bit in bits:
                part = jnp.concatenate([part, swap(part, "row", 1 << bit, n_row)])
            return part.astype(F32)

        if chunks > 1:
            low, high = list(range(n_stripes // 2)), list(range(n_stripes // 2, n_stripes))
            kept, b_sent, val_density, fixed = load()
            b = [kept], b_sent
            kept, sent, fixed = pair(fixed, val_density, [b_sent])
            b = run(3, 0, 1, *b)
            kept, a_got, a_sent = quarters(kept, send(0, 0, sent), orders[0][1:3])
            before, fixed = begin(2, low, fixed, [b[1], *a_sent])
            m, density = end(high, fixed, before, [])
            m_kept, m_got, m_sent = quarters([m[0]], send(2, 0, m[1]), orders[2][1:3])
            kept, (sent,) = fold(kept, a_got, [steps[0][3]] * 2, [[0, 1]] * 3)
            b = run(3, 1, col_bits, *b)
            b_kept, b_sent = last(density, b[1], [])
            b = [b_kept], b_sent
            when = [b_sent]
            axis_steps = len(steps[3]) - 1
            for s in range(col_bits + 1, axis_steps):
                axis, bit, _ = steps[3][s]
                got = swap(b[1], axis, 1 << bit, sizes[axis])
                kept_b, (sent_b,) = fold(b[0], [got], [steps[3][s + 1]])
                b = kept_b, sent_b
            _, a_sums = run(0, 3, n_steps, kept, sent)
            m_kept, m_sent = fold(m_kept, m_got, [steps[2][3]], [[0]] * 3)
            _, m_sums = run(2, 3, n_steps, m_kept, m_sent[0])
            up, down = order + [0], order[::-1] + [0]
            arrays = [gather(a_sums, down), gather(b[1], up), gather(m_sums, up)]
            gathers = [(down, [0, 1]), (up, [3]), (up, [2])]
        else:
            kept, sent = single()
            when = []
            _, late = run(0, 0, n_steps, [kept], sent)
            late_bits = order[::-1] + [0]
            arrays, gathers = [gather(late, late_bits)], [(late_bits, [0])]
        gathers = [(bits, [(starts[k], width // n_row, orders[k]) for k in ks]) for bits, ks in gathers]

        own = con_pairs.shape[0] // n_row
        pick = pl.pallas_call(
            functools.partial(hot_kernel, n_col, count, len(when)),
            in_specs=[smem, vmem] + [anywhere] * len(when),
            out_specs=vmem,
            out_shape=pltpu.VMEM((unordered, own), BF16),
            compiler_params=params(8),
            name="hot",
        )(place, con_pairs.T, *when)
        return pl.pallas_call(
            functools.partial(pick_kernel, n_col, float(grid ** (-0.5)), gathers),
            in_specs=[smem] + [vmem] * (1 + len(arrays)),
            out_specs=vmem,
            out_shape=jax.ShapeDtypeStruct((own, per_col), F32),
            scratch_shapes=[pltpu.VMEM((per_col, unordered), F32)],
            compiler_params=params(20),
            name="pick",
        )(place, pick, *arrays)

    in_specs = (P("row", "col"), P(None, "col"), P(), P(), P())

    return jax.shard_map(per_device, mesh=mesh, in_specs=in_specs, out_specs=P("row", "col"), check_vma=False)
```

```python
import functools

import jax
import jax.numpy as jnp
from jax import lax
from jax.experimental import pallas as pl
from jax.experimental.pallas import tpu as pltpu
from jax.sharding import PartitionSpec as P


CHUNKS = 4

F32, BF16 = jnp.float32, jnp.bfloat16
CONTRACT_MINOR = (((1,), (1,)), ((), ()))


def one_hot_columns(index, count):
    numbers = lax.broadcasted_iota(jnp.int32, (count, index.shape[1]), 0)
    return jnp.where(numbers == index, 1.0, 0.0)


def groups(ref, n_col, start, width):
    each = ref.shape[0] // n_col
    return jnp.concatenate([ref[z * each + start : z * each + start + width, :] for z in range(n_col)])


def build_val(first, second, val_ref, val_density):
    grid = val_ref.shape[1]
    step = min(2048, grid)

    @pl.loop(0, grid // step)
    def _(i):
        at = pl.ds(pl.multiple_of(i * step, step), step)
        orbitals = val_ref[:, at]
        a = jnp.dot(first, orbitals, preferred_element_type=F32)
        b = jnp.dot(second, orbitals, preferred_element_type=F32)
        val_density[:, at] = (a * b).astype(BF16)


def build_con(con, rolled, density):
    count, columns = con.shape
    wide = min(512, columns)
    apart = density.shape[0] // count

    @pl.loop(0, columns // wide)
    def _(i):
        at = pl.ds(pl.multiple_of(i * wide, wide), wide)
        one = con[:, at].astype(F32)
        for shift in range(8):
            moved = one if shift == 0 else jnp.concatenate([one[shift:], one[:shift]])
            rolled[0:count, :] = moved
            rolled[count : 2 * count, :] = moved
            for d in range(shift, apart, 8):
                other = rolled[d - shift : d - shift + count, :]
                density[d * count : (d + 1) * count, at] = (one * other).astype(BF16)


def product(numbers, w, density, val_density):
    stripe = w[0].shape[0]
    t = [lax.dot_general(val_density[...], w[s][...], CONTRACT_MINOR, preferred_element_type=F32).astype(BF16) for s in numbers]
    rows = slice(numbers[0] * stripe, (numbers[-1] + 1) * stripe)
    return lax.dot_general(jnp.concatenate(t, axis=1), density[:, rows], CONTRACT_MINOR, preferred_element_type=F32)


def hand_out(n_col, mine, acc, kept, sent):
    half = kept[0].shape[0] // n_col
    for c, own in enumerate(kept):
        for z in range(n_col):
            first = (z * len(kept) + c) * 2
            to = slice(z * half, (z + 1) * half)
            own[to, :] = acc[pl.ds(pl.multiple_of((first + mine) * half, half), half), :]
            to = slice((c * n_col + z) * half, (c * n_col + z + 1) * half)
            sent[to, :] = acc[pl.ds(pl.multiple_of((first + 1 - mine) * half, half), half), :].astype(BF16)


def deal(index, ways, each, size, source, base, outs, starts):
    for flip, (out, start) in enumerate(zip(outs, starts)):
        for g in range(each):
            at = base + g * ways * size + (index ^ flip) * size
            rows = source[pl.ds(pl.multiple_of(at, size), size), :]
            out[start + g * size : start + (g + 1) * size, :] = rows.astype(out.dtype)


def fetch_all(n_col, n_stripes, place, hbm, vmem, sems, in_sems):
    pairs, val, con_all, w_hbm = hbm
    pairs_here, val_here, con, w = vmem
    columns, stripe = con.shape[1], w[0].shape[0]
    mine = pl.ds(pl.multiple_of((place[0] // n_col) * columns, columns), columns)
    fetches = [
        pltpu.make_async_copy(pairs, pairs_here, in_sems.at[0]),
        pltpu.make_async_copy(val, val_here, in_sems.at[1]),
        pltpu.make_async_copy(con_all.at[:, mine], con, in_sems.at[2]),
    ]
    fetches += [
        pltpu.make_async_copy(w_hbm.at[pl.ds(s * stripe, stripe), :], w[s], sems.at[s]) for s in range(n_stripes)
    ]
    for fetch in fetches[:3]:
        fetch.start()
    return fetches[:3], fetches[3:]


def make_hot(pairs, hot1, hot2):
    hot1[...] = one_hot_columns(pairs[0:1, :], hot1.shape[1]).T.astype(BF16)
    hot2[...] = one_hot_columns(pairs[1:2, :], hot2.shape[1]).T.astype(BF16)


def single_kernel(n_col, n_stripes, place, pairs, val, con_all, w_hbm, kept, sent, val_density, acc, density, hot1, hot2, pairs_here, val_here, con, rolled, sems, in_sems, *w):
    inputs, stripes = fetch_all(n_col, n_stripes, place, (pairs, val, con_all, w_hbm), (pairs_here, val_here, con, w), sems, in_sems)
    for fetch in stripes:
        fetch.start()
    for fetch in inputs:
        fetch.wait()
    make_hot(pairs_here, hot1, hot2)
    build_val(hot1[...], hot2[...], val_here, val_density)
    build_con(con, rolled, density)
    for fetch in stripes:
        fetch.wait()
    acc[...] = product(list(range(n_stripes)), w, density, val_density)
    hand_out(n_col, place[0] // n_col % 2, acc, [kept], sent)


def load_kernel(n_col, start, width, n_stripes, place, pairs, val, con_all, w_hbm, kept, *refs):
    sent, (val_a, *refs) = refs[: n_col - 1], refs[n_col - 1 :]
    w, refs = refs[:n_stripes], refs[n_stripes:]
    density, hot1, hot2, val_b, acc, pairs_here, val_here, con, rolled, sems, in_sems = refs
    inputs, stripes = fetch_all(n_col, n_stripes, place, (pairs, val, con_all, w_hbm), (pairs_here, val_here, con, w), sems, in_sems)
    inputs[0].wait()
    inputs[1].wait()
    for fetch in stripes:
        fetch.start()
    make_hot(pairs_here, hot1, hot2)
    build_val(groups(hot1, n_col, start, width), groups(hot2, n_col, start, width), val_here, val_b)
    build_val(groups(hot1, n_col, 0, 2 * width), groups(hot2, n_col, 0, 2 * width), val_here, val_a)
    inputs[2].wait()
    build_con(con, rolled, density)
    for s, fetch in enumerate(stripes):
        fetch.wait()
        stripe = w[s].shape[0]
        t = lax.dot_general(val_b[...], w[s][...], CONTRACT_MINOR, preferred_element_type=F32)
        acc[:, s * stripe : (s + 1) * stripe] = t
    deal(place[0] % n_col, n_col, 1, width, acc, 0, [kept, *sent], [0] * n_col)


def pair_kernel(n_col, n_stripes, n_after, place, *refs):
    w, refs = refs[:n_stripes], refs[n_stripes:]
    (density, val_density), refs = refs[:2], refs[2 + n_after :]
    kept, sent, acc = refs[:2], refs[2], refs[-1]
    at_once = 2 - n_stripes % 2
    for s in range(0, n_stripes, at_once):
        part = product(list(range(s, s + at_once)), w, density, val_density)
        if s == 0:
            acc[...] = part
        else:
            acc[...] += part
    hand_out(n_col, place[0] // n_col % 2, acc, kept, sent)


def val_kernel(n_col, start, width, n_after, hot1, hot2, val, *refs):
    build_val(groups(hot1, n_col, start, width), groups(hot2, n_col, start, width), val, refs[n_after])


def grid_kernel(n_stripes, n_after, *refs):
    w, val_density, t = refs[:n_stripes], refs[n_stripes], refs[n_stripes + 1 + n_after]
    stripe = w[0].shape[0]
    for s in range(n_stripes):
        part = lax.dot_general(val_density[...], w[s][...], CONTRACT_MINOR, preferred_element_type=F32)
        t[:, s * stripe : (s + 1) * stripe] = part.astype(BF16)


def con_kernel(n_col, place, density, t_m, t_b, kept_m, kept_b, sent, acc):
    both = jnp.concatenate([t_m[...], t_b[...]])
    acc[...] = lax.dot_general(both, density[...], CONTRACT_MINOR, preferred_element_type=F32)
    mine = place[0] // n_col % 2
    rows, size = t_m.shape[0], t_b.shape[0] // 2
    deal(mine, 2, n_col, size, acc, 0, [kept_m, sent], [0, 0])
    deal(mine, 2, 1, size, acc, rows, [kept_b, sent], [0, rows // 2])


def spread_kernel(n_col, axis, bits, eaches, offsets, n_got, place, *refs):
    n, ways = len(eaches), 1 << len(bits)
    kept, got, refs = refs[:n], refs[n : n + n_got], refs[n + n_got :]
    kept_out, sent, part = refs[:n], refs[n:-1], refs[-1]
    me = place[0] // n_col if axis == "row" else place[0] % n_col
    index = sum(((me >> bit) & 1) << (len(bits) - 1 - k) for k, bit in enumerate(bits))
    to = 0
    for c, (each, at) in enumerate(zip(eaches, offsets)):
        rows = kept[c].shape[0]
        total = kept[c][...]
        for arrived in got:
            total = total + arrived[at : at + rows, :].astype(F32)
        part[0:rows, :] = total
        deal(index, ways, each, rows // ways // each, part, 0, [kept_out[c], *sent], [0] + [to] * (ways - 1))
        to += rows // ways


def sum_kernel(offsets, *refs):
    kept, got, out = refs[: len(offsets)], refs[len(offsets) : -1], refs[-1]
    to = 0
    for part, at in zip(kept, offsets):
        rows = part.shape[0]
        total = part[...]
        for arrived in got:
            total = total + arrived[at : at + rows, :].astype(F32)
        out[to : to + rows, :] = total.astype(BF16)
        to += rows


def fold_kernel(n_col, targets, got_groups, sent_groups, place, *refs):
    n = len(targets)
    kept, got = refs[:n], refs[n : n + len(got_groups)]
    out = refs[n + len(got_groups) :]
    halves, sent = out[: len(out) - len(sent_groups)], out[len(out) - len(sent_groups) :]
    source, sink = {}, {}
    for array, group in zip(got, got_groups):
        at = 0
        for c in group:
            source.setdefault(c, []).append((array, at))
            at += kept[c].shape[0]
    for array, group in zip(sent, sent_groups):
        at = 0
        for c in group:
            sink[c] = array, at
            at += kept[c].shape[0] // (2 if targets[c] else 1)
    for c, target in enumerate(targets):
        rows, (other, to) = kept[c].shape[0], sink[c]

        def part(first, size, c=c):
            total = kept[c][first : first + size, :]
            for array, at in source[c]:
                total = total + array[at + first : at + first + size, :].astype(F32)
            return total

        if target is None:
            other[to : to + rows, :] = part(0, rows).astype(BF16)
            continue
        axis, bit, each = target
        me = place[0] // n_col if axis == "row" else place[0] % n_col
        high = (me >> bit) % 2 == 1
        half = rows // each // 2
        for z in range(each):
            a, b = 2 * z * half, (2 * z + 1) * half
            low_part, high_part = part(a, half), part(b, half)
            halves[c][z * half : (z + 1) * half, :] = jnp.where(high, high_part, low_part)
            other[to + z * half : to + (z + 1) * half, :] = jnp.where(high, low_part, high_part).astype(BF16)


def hot_kernel(n_col, count, n_after, place, pairs, *refs):
    pick = refs[n_after]
    own = pick.shape[1]
    me = place[0] // n_col
    if own % 128:
        every = pairs[...]
        asked = functools.reduce(
            lambda a, i: jnp.where(me == i, every[:, i * own : (i + 1) * own], a), range(pairs.shape[1] // own), every[:, :own]
        )
    else:
        asked = pairs[:, pl.ds(pl.multiple_of(me * own, own), own)]
    c, other = asked[0:1], asked[1:2]
    apart = jnp.where(other >= c, other - c, other - c + count)
    row = jnp.where(apart <= count // 2, apart * count + c, (count - apart) * count + other)
    pick[...] = one_hot_columns(row, pick.shape[0]).astype(BF16)


def pick_kernel(n_col, scale, gathers, place, pick, *refs):
    arrays, (out, found, turned) = refs[: len(gathers)], refs[len(gathers) :]
    me = place[0] // n_col
    whole = jnp.concatenate([array[...] for array in arrays])
    found[...] = jnp.dot(whole, pick[...], preferred_element_type=F32) * scale
    base = 0
    for array, (steps, chunks) in zip(arrays, gathers):
        each = sum(rows for _, rows, _ in chunks)
        for j in range(array.shape[0] // each):
            block = sum((((me ^ j) >> bit) % 2) << s for s, bit in enumerate(steps))
            used = 0
            for start, rows, order in chunks:
                spot = sum(((j >> bit) & 1) << (len(order) - 1 - s) for s, bit in enumerate(order))
                to = start + spot * rows
                turned[to : to + rows, :] = found[pl.ds(base + block * each + used, rows), :]
                used += rows
        base += array.shape[0]
    out[...] = turned[...].T


def swap(x, axis, bits, size):
    return lax.ppermute(x, axis, [(i, i ^ bits) for i in range(size)])


def solution(mesh):
    n_row, n_col = mesh.shape["row"], mesh.shape["col"]
    row_bits, col_bits = n_row.bit_length() - 1, n_col.bit_length() - 1

    def per_device(screened, val_orbitals, con_orbitals, val_pairs, con_pairs):
        own_rows, own_columns = screened.shape
        count, grid = con_orbitals.shape
        n_val = val_orbitals.shape[0]
        blocks = count // 2 + 1
        while blocks * count % 128:
            blocks += 1
        unordered = blocks * count
        n_pairs = val_pairs.shape[0]
        per_col = n_pairs // n_col
        chunks = CHUNKS if n_pairs >= 8 * CHUNKS * n_row * n_col and row_bits == 3 else 1
        width = per_col // chunks
        starts = [k * width for k in range(chunks)]
        place = (lax.axis_index("row") * n_col + lax.axis_index("col")).astype(jnp.int32)[None]
        smem = pl.BlockSpec(memory_space=pltpu.SMEM)
        vmem = pl.BlockSpec(memory_space=pltpu.VMEM)
        anywhere = pl.BlockSpec(memory_space=pl.ANY)
        hbm = pl.BlockSpec(memory_space=pltpu.HBM)

        def params(mib):
            return pltpu.CompilerParams(vmem_limit_bytes=mib << 20)

        def outs(rows):
            return [pltpu.VMEM((rows, unordered), F32), pltpu.VMEM((rows, unordered), BF16)]

        stripe = min(512, own_rows)
        n_stripes = own_rows // stripe
        held = [pltpu.VMEM((stripe, own_columns), BF16)] * n_stripes + [pltpu.VMEM((unordered, own_rows), BF16)]
        hots = [pltpu.VMEM((n_pairs, n_val), BF16)] * 2
        n_held = n_stripes + 1
        arguments = (place, *[pltpu.with_memory_space_constraint(x, pltpu.HBM) for x in (val_pairs.T, val_orbitals, con_orbitals, screened)])
        inputs = [
            pltpu.VMEM((2, n_pairs), jnp.int32),
            pltpu.VMEM((n_val, own_columns), BF16),
            pltpu.VMEM((count, own_rows), BF16),
            pltpu.VMEM((2 * count, min(512, own_rows)), F32),
            pltpu.SemaphoreType.DMA((n_stripes,)),
            pltpu.SemaphoreType.DMA((3,)),
        ]
        n = n_col * width

        def single():
            return pl.pallas_call(
                functools.partial(single_kernel, n_col, n_stripes),
                in_specs=[smem] + [hbm] * 4,
                out_specs=[vmem] * 2,
                out_shape=outs(n // 2),
                scratch_shapes=[pltpu.VMEM((n, own_columns), BF16), pltpu.VMEM((n, unordered), F32), held[-1], *hots, *inputs, *held[:-1]],
                compiler_params=params(40),
                name="single",
            )(*arguments)

        def call(kernel, in_specs, out_shape, operands, after=(), scratch=(), aliases={}, mib=8, flops=0):
            return pl.pallas_call(
                kernel,
                in_specs=in_specs + [anywhere] * len(after),
                out_specs=[vmem] * len(out_shape),
                out_shape=out_shape,
                scratch_shapes=list(scratch),
                input_output_aliases=aliases,
                compiler_params=params(mib),
                cost_estimate=pl.CostEstimate(flops=flops, bytes_accessed=1 << 20, transcendentals=0),
            )(*operands, *after)

        def load():
            kept, *rest = call(
                functools.partial(load_kernel, n_col, starts[3], width, n_stripes),
                [smem] + [hbm] * 4,
                [pltpu.VMEM((width, own_rows), F32)]
                + [pltpu.VMEM((width, own_rows), BF16)] * (n_col - 1)
                + [pltpu.VMEM((2 * n, own_columns), BF16), *held, *hots],
                arguments,
                scratch=[pltpu.VMEM((n, own_columns), BF16), pltpu.VMEM((n, own_rows), F32), *inputs],
                mib=12,
                flops=2 * n * own_rows * own_columns,
            )
            return kept, rest[: n_col - 1], rest[n_col - 1], rest[n_col : n_col + n_held], rest[n_col + n_held :]

        def pair(fixed, val_density, after):
            out = call(
                functools.partial(pair_kernel, n_col, n_stripes, len(after)),
                [smem] + [vmem] * (n_held + 1),
                [outs(n // 2)[0]] * 2 + [outs(n)[1]] + held,
                (place, *fixed, val_density),
                after,
                [pltpu.VMEM((2 * n, unordered), F32)],
                {1 + i: 3 + i for i in range(n_held)},
                12,
                4 * n * own_rows * (own_columns + unordered),
            )
            return list(out[:2]), out[2], list(out[3:])

        def scatter(sent, axis, bits):
            got = []
            for flip, x in enumerate(sent, 1):
                mask = sum(((flip >> (len(bits) - 1 - k)) & 1) << bit for k, bit in enumerate(bits))
                got.append(swap(x, axis, mask, mesh.shape[axis]))
            return got

        def spread(kept, got, axis, bits, eaches, offsets):
            ways = 1 << len(bits)
            rows = [k.shape[0] // ways for k in kept]
            out = call(
                functools.partial(spread_kernel, n_col, axis, bits, eaches, offsets, len(got)),
                [smem] + [vmem] * (len(kept) + len(got)),
                [pltpu.VMEM((r, unordered), F32) for r in rows] + [pltpu.VMEM((sum(rows), unordered), BF16)] * (ways - 1),
                (place, *kept, *got),
                scratch=[pltpu.VMEM((max(rows) * ways, unordered), F32)],
                mib=6,
            )
            return list(out[: len(kept)]), list(out[len(kept) :])

        def total(kept, got, offsets):
            return call(
                functools.partial(sum_kernel, offsets),
                [vmem] * (len(kept) + len(got)),
                [pltpu.VMEM((sum(k.shape[0] for k in kept), kept[0].shape[1]), BF16)],
                (*kept, *got),
                mib=6,
            )[0]

        def fold(kept, got, targets, got_groups=None, sent_groups=None):
            everything = [list(range(len(kept)))]
            got_groups, sent_groups = got_groups or everything, sent_groups or everything
            rows = [k.shape[0] // (2 if t else 1) for k, t in zip(kept, targets)]
            minor = kept[0].shape[1]
            shapes = [pltpu.VMEM((r, minor), F32) for r, t in zip(rows, targets) if t]
            n_kept = len(shapes)
            shapes += [pltpu.VMEM((sum(rows[c] for c in g), minor), BF16) for g in sent_groups]
            out = pl.pallas_call(
                functools.partial(fold_kernel, n_col, targets, got_groups, sent_groups),
                in_specs=[smem] + [vmem] * (len(kept) + len(got)),
                out_specs=[vmem] * len(shapes),
                out_shape=shapes,
                compiler_params=params(4),
            )(place, *kept, *got)
            return list(out[:n_kept]), list(out[n_kept:])

        order = list(range(1, row_bits))
        orders = [[0] + order for _ in range(chunks)]
        steps = [
            [("row", bit, n_col) for bit in orders[0]] + [("col", bit, n_col >> (bit + 1)) for bit in range(col_bits)] + [None]
        ]
        n_steps = row_bits + col_bits
        sizes = {"row": n_row, "col": n_col}

        def send(k, at, sent):
            axis, bit, _ = steps[k][at]
            return swap(sent, axis, 1 << bit, sizes[axis])

        def run(k, at, until, kept, sent):
            for s in range(at, until):
                got = send(k, s, sent)
                kept, (sent,) = fold(kept, [got], [steps[k][s + 1]] * len(kept))
            return kept, sent

        def gather(part, steps):
            for bits in steps:
                flips = [1 << bits[0]] if len(bits) == 1 else [1 << bits[0], 1 << bits[1], 1 << bits[0] | 1 << bits[1]]
                got = [swap(part, "row", flip, n_row) for flip in flips]
                part = jnp.concatenate([part, *got])
            return part

        if chunks > 1:
            cols = tuple(reversed(range(col_bits)))
            half = n // 2
            b_kept, b_sent, val_a, fixed, hot = load()
            b_got = scatter(b_sent, "col", cols)
            a_kept, a_sent, fixed = pair(fixed, val_a, b_sent)
            a_got = [swap(a_sent, "row", 1, n_row)]
            when = [a_sent]
            val_m = call(
                functools.partial(val_kernel, n_col, starts[2], width, 1), [vmem] * 3,
                [pltpu.VMEM((n, own_columns), BF16)], (*hot, val_orbitals), when, mib=6,
            )[0]
            a_kept, a_sent = spread(a_kept, a_got, "row", tuple(order), [n_col] * 2, [0, half])
            a_got = scatter(a_sent, "row", order)
            t_m = call(
                functools.partial(grid_kernel, n_stripes, len(a_sent)), [vmem] * (n_stripes + 1),
                [pltpu.VMEM((n, own_rows), BF16)], (*fixed[:-1], val_m), a_sent, mib=8, flops=2 * n * own_rows * own_columns,
            )[0]
            t_b = total([b_kept], b_got, [0])
            m_kept, b_kept, sent = call(
                functools.partial(con_kernel, n_col), [smem] + [vmem] * 3,
                [outs(half)[0], outs(width // 2)[0], outs(half + width // 2)[1]], (place, fixed[-1], t_m, t_b),
                scratch=[pltpu.VMEM((n + width, unordered), F32)], mib=12, flops=2 * (n + width) * own_rows * unordered,
            )
            got = [swap(sent, "row", 1, n_row)]
            (m_kept, b_kept), sent = spread([m_kept, b_kept], got, "row", tuple(order), [n_col, 1], [0, half])
            mb_got = scatter(sent, "row", order)
            a_kept, a_sent = spread(a_kept, a_got, "col", cols, [1, 1], [0, a_kept[0].shape[0]])
            a_got = scatter(a_sent, "col", cols)
            rows = m_kept.shape[0]
            m_kept, m_sent = spread([m_kept], mb_got, "col", cols, [1], [0])
            m_got = scatter(m_sent, "col", cols)
            b_sums = total([b_kept], mb_got, [rows])
            a_sums = total(a_kept, a_got, [0, a_kept[0].shape[0]])
            m_sums = total(m_kept, m_got, [0])
            square = [order, [0]]
            arrays = [gather(jnp.concatenate([a_sums, b_sums]), square), gather(m_sums, square)]
            gathers = [(order + [0], [0, 1, 3]), (order + [0], [2])]
        else:
            kept, sent = single()
            when = []
            _, late = run(0, 0, n_steps, [kept], sent)
            late_bits = order[::-1] + [0]
            arrays, gathers = [gather(late, [[bit] for bit in late_bits])], [(late_bits, [0])]
        gathers = [(bits, [(starts[k], width // n_row, orders[k]) for k in ks]) for bits, ks in gathers]

        own = con_pairs.shape[0] // n_row
        pick = pl.pallas_call(
            functools.partial(hot_kernel, n_col, count, len(when)),
            in_specs=[smem, vmem] + [anywhere] * len(when),
            out_specs=vmem,
            out_shape=pltpu.VMEM((unordered, own), BF16),
            compiler_params=params(8),
            name="hot",
        )(place, con_pairs.T, *when)
        return pl.pallas_call(
            functools.partial(pick_kernel, n_col, float(grid ** (-0.5)), gathers),
            in_specs=[smem] + [vmem] * (1 + len(arrays)),
            out_specs=vmem,
            out_shape=jax.ShapeDtypeStruct((own, per_col), F32),
            scratch_shapes=[pltpu.VMEM((per_col, own), F32)] * 2,
            compiler_params=params(20),
            name="pick",
        )(place, pick, *arrays)

    in_specs = (P("row", "col"), P(None, "col"), P(), P(), P())

    return jax.shard_map(per_device, mesh=mesh, in_specs=in_specs, out_specs=P("row", "col"), check_vma=False)
```

```python
import functools

import jax
import jax.numpy as jnp
from jax import lax
from jax.experimental import pallas as pl
from jax.experimental.pallas import tpu as pltpu
from jax.sharding import PartitionSpec as P


CHUNKS = 4

F32, BF16 = jnp.float32, jnp.bfloat16
CONTRACT_MINOR = (((1,), (1,)), ((), ()))


def one_hot_columns(index, count):
    numbers = lax.broadcasted_iota(jnp.int32, (count, index.shape[1]), 0)
    return jnp.where(numbers == index, 1.0, 0.0)


def groups(ref, n_col, start, width):
    each = ref.shape[0] // n_col
    return jnp.concatenate([ref[z * each + start : z * each + start + width, :] for z in range(n_col)])


def build_val(first, second, val_ref, val_density):
    grid = val_ref.shape[1]
    step = min(2048, grid)

    @pl.loop(0, grid // step)
    def _(i):
        at = pl.ds(pl.multiple_of(i * step, step), step)
        orbitals = val_ref[:, at]
        a = jnp.dot(first, orbitals, preferred_element_type=F32)
        b = jnp.dot(second, orbitals, preferred_element_type=F32)
        val_density[:, at] = (a * b).astype(BF16)


def build_con(con, rolled, density):
    count, columns = con.shape
    wide = min(512, columns)
    apart = density.shape[0] // count

    @pl.loop(0, columns // wide)
    def _(i):
        at = pl.ds(pl.multiple_of(i * wide, wide), wide)
        one = con[:, at].astype(F32)
        for shift in range(8):
            moved = one if shift == 0 else jnp.concatenate([one[shift:], one[:shift]])
            rolled[0:count, :] = moved
            rolled[count : 2 * count, :] = moved
            for d in range(shift, apart, 8):
                other = rolled[d - shift : d - shift + count, :]
                density[d * count : (d + 1) * count, at] = (one * other).astype(BF16)


def product(numbers, w, density, val_density):
    stripe = w[0].shape[0]
    t = [lax.dot_general(val_density[...], w[s][...], CONTRACT_MINOR, preferred_element_type=F32).astype(BF16) for s in numbers]
    rows = slice(numbers[0] * stripe, (numbers[-1] + 1) * stripe)
    return lax.dot_general(jnp.concatenate(t, axis=1), density[:, rows], CONTRACT_MINOR, preferred_element_type=F32)


def hand_out(n_col, mine, acc, kept, sent):
    half = kept[0].shape[0] // n_col
    for c, own in enumerate(kept):
        for z in range(n_col):
            first = (z * len(kept) + c) * 2
            to = slice(z * half, (z + 1) * half)
            own[to, :] = acc[pl.ds(pl.multiple_of((first + mine) * half, half), half), :]
            to = slice((c * n_col + z) * half, (c * n_col + z + 1) * half)
            sent[to, :] = acc[pl.ds(pl.multiple_of((first + 1 - mine) * half, half), half), :].astype(BF16)


def deal(index, ways, each, size, source, base, outs, starts):
    for flip, (out, start) in enumerate(zip(outs, starts)):
        for g in range(each):
            at = base + g * ways * size + (index ^ flip) * size
            rows = source[pl.ds(pl.multiple_of(at, size), size), :]
            out[start + g * size : start + (g + 1) * size, :] = rows.astype(out.dtype)


def fetch_all(n_col, n_stripes, place, hbm, vmem, sems, in_sems):
    pairs, val, con_all, w_hbm = hbm
    pairs_here, val_here, con, w = vmem
    columns, stripe = con.shape[1], w[0].shape[0]
    mine = pl.ds(pl.multiple_of((place[0] // n_col) * columns, columns), columns)
    fetches = [
        pltpu.make_async_copy(pairs, pairs_here, in_sems.at[0]),
        pltpu.make_async_copy(val, val_here, in_sems.at[1]),
        pltpu.make_async_copy(con_all.at[:, mine], con, in_sems.at[2]),
    ]
    fetches += [
        pltpu.make_async_copy(w_hbm.at[pl.ds(s * stripe, stripe), :], w[s], sems.at[s]) for s in range(n_stripes)
    ]
    for fetch in fetches[:3]:
        fetch.start()
    return fetches[:3], fetches[3:]


def make_hot(pairs, hot1, hot2):
    hot1[...] = one_hot_columns(pairs[0:1, :], hot1.shape[1]).T.astype(BF16)
    hot2[...] = one_hot_columns(pairs[1:2, :], hot2.shape[1]).T.astype(BF16)


def single_kernel(n_col, n_stripes, place, pairs, val, con_all, w_hbm, kept, sent, val_density, acc, density, hot1, hot2, pairs_here, val_here, con, rolled, sems, in_sems, *w):
    inputs, stripes = fetch_all(n_col, n_stripes, place, (pairs, val, con_all, w_hbm), (pairs_here, val_here, con, w), sems, in_sems)
    for fetch in stripes:
        fetch.start()
    for fetch in inputs:
        fetch.wait()
    make_hot(pairs_here, hot1, hot2)
    build_val(hot1[...], hot2[...], val_here, val_density)
    build_con(con, rolled, density)
    for fetch in stripes:
        fetch.wait()
    acc[...] = product(list(range(n_stripes)), w, density, val_density)
    hand_out(n_col, place[0] // n_col % 2, acc, [kept], sent)


def load_kernel(n_col, start, width, n_stripes, place, pairs, val, con_all, w_hbm, kept, *refs):
    sent, (val_a, *refs) = refs[: n_col - 1], refs[n_col - 1 :]
    w, refs = refs[:n_stripes], refs[n_stripes:]
    density, hot1, hot2, val_b, acc, pairs_here, val_here, con, rolled, sems, in_sems = refs
    inputs, stripes = fetch_all(n_col, n_stripes, place, (pairs, val, con_all, w_hbm), (pairs_here, val_here, con, w), sems, in_sems)
    inputs[0].wait()
    inputs[1].wait()
    for fetch in stripes:
        fetch.start()
    make_hot(pairs_here, hot1, hot2)
    build_val(groups(hot1, n_col, start, width), groups(hot2, n_col, start, width), val_here, val_b)
    build_val(groups(hot1, n_col, 0, 2 * width), groups(hot2, n_col, 0, 2 * width), val_here, val_a)
    inputs[2].wait()
    build_con(con, rolled, density)
    for s, fetch in enumerate(stripes):
        fetch.wait()
        stripe = w[s].shape[0]
        t = lax.dot_general(val_b[...], w[s][...], CONTRACT_MINOR, preferred_element_type=F32)
        acc[:, s * stripe : (s + 1) * stripe] = t
    deal(place[0] % n_col, n_col, 1, width, acc, 0, [kept, *sent], [0] * n_col)


def pair_kernel(n_col, n_stripes, n_after, place, *refs):
    w, refs = refs[:n_stripes], refs[n_stripes:]
    (density, val_density), refs = refs[:2], refs[2 + n_after :]
    kept, sent, acc = refs[:2], refs[2], refs[-1]
    at_once = 2 - n_stripes % 2
    for s in range(0, n_stripes, at_once):
        part = product(list(range(s, s + at_once)), w, density, val_density)
        if s == 0:
            acc[...] = part
        else:
            acc[...] += part
    hand_out(n_col, place[0] // n_col % 2, acc, kept, sent)


def val_kernel(n_col, start, width, n_after, hot1, hot2, val, *refs):
    build_val(groups(hot1, n_col, start, width), groups(hot2, n_col, start, width), val, refs[n_after])


def grid_kernel(n_stripes, n_after, *refs):
    w, val_density, t = refs[:n_stripes], refs[n_stripes], refs[n_stripes + 1 + n_after]
    stripe = w[0].shape[0]
    for s in range(n_stripes):
        part = lax.dot_general(val_density[...], w[s][...], CONTRACT_MINOR, preferred_element_type=F32)
        t[:, s * stripe : (s + 1) * stripe] = part.astype(BF16)


def con_kernel(n_col, first, size_of_cut, n_same, place, density, t_m, t_b, kept_m, kept_b, sent, *refs):
    acc = refs[n_same]
    both = jnp.concatenate([t_m[...], t_b[...]])
    rows_of_cut = density[first : first + size_of_cut, :]
    acc[...] = lax.dot_general(both, rows_of_cut, CONTRACT_MINOR, preferred_element_type=F32)
    mine = place[0] // n_col % 2
    rows, size = t_m.shape[0], t_b.shape[0] // 2
    deal(mine, 2, n_col, size, acc, 0, [kept_m, sent], [0, 0])
    deal(mine, 2, 1, size, acc, rows, [kept_b, sent], [0, rows // 2])


def spread_kernel(n_col, axis, bits, eaches, offsets, n_got, place, *refs):
    n, ways = len(eaches), 1 << len(bits)
    kept, got, refs = refs[:n], refs[n : n + n_got], refs[n + n_got :]
    kept_out, sent, part = refs[:n], refs[n:-1], refs[-1]
    me = place[0] // n_col if axis == "row" else place[0] % n_col
    index = sum(((me >> bit) & 1) << (len(bits) - 1 - k) for k, bit in enumerate(bits))
    to = 0
    for c, (each, at) in enumerate(zip(eaches, offsets)):
        rows = kept[c].shape[0]
        total = kept[c][...]
        for arrived in got:
            total = total + arrived[at : at + rows, :].astype(F32)
        part[0:rows, :] = total
        deal(index, ways, each, rows // ways // each, part, 0, [kept_out[c], *sent], [0] + [to] * (ways - 1))
        to += rows // ways


def sum_kernel(offsets, *refs):
    kept, got, out = refs[: len(offsets)], refs[len(offsets) : -1], refs[-1]
    to = 0
    for part, at in zip(kept, offsets):
        rows = part.shape[0]
        total = part[...]
        for arrived in got:
            total = total + arrived[at : at + rows, :].astype(F32)
        out[to : to + rows, :] = total.astype(BF16)
        to += rows


def fold_kernel(n_col, targets, got_groups, sent_groups, place, *refs):
    n = len(targets)
    kept, got = refs[:n], refs[n : n + len(got_groups)]
    out = refs[n + len(got_groups) :]
    halves, sent = out[: len(out) - len(sent_groups)], out[len(out) - len(sent_groups) :]
    source, sink = {}, {}
    for array, group in zip(got, got_groups):
        at = 0
        for c in group:
            source.setdefault(c, []).append((array, at))
            at += kept[c].shape[0]
    for array, group in zip(sent, sent_groups):
        at = 0
        for c in group:
            sink[c] = array, at
            at += kept[c].shape[0] // (2 if targets[c] else 1)
    for c, target in enumerate(targets):
        rows, (other, to) = kept[c].shape[0], sink[c]

        def part(first, size, c=c):
            total = kept[c][first : first + size, :]
            for array, at in source[c]:
                total = total + array[at + first : at + first + size, :].astype(F32)
            return total

        if target is None:
            other[to : to + rows, :] = part(0, rows).astype(BF16)
            continue
        axis, bit, each = target
        me = place[0] // n_col if axis == "row" else place[0] % n_col
        high = (me >> bit) % 2 == 1
        half = rows // each // 2
        for z in range(each):
            a, b = 2 * z * half, (2 * z + 1) * half
            low_part, high_part = part(a, half), part(b, half)
            halves[c][z * half : (z + 1) * half, :] = jnp.where(high, high_part, low_part)
            other[to + z * half : to + (z + 1) * half, :] = jnp.where(high, low_part, high_part).astype(BF16)


def hot_kernel(n_col, count, n_after, place, pairs, *refs):
    pick = refs[n_after]
    own = pick.shape[1]
    me = place[0] // n_col
    if own % 128:
        every = pairs[...]
        asked = functools.reduce(
            lambda a, i: jnp.where(me == i, every[:, i * own : (i + 1) * own], a), range(pairs.shape[1] // own), every[:, :own]
        )
    else:
        asked = pairs[:, pl.ds(pl.multiple_of(me * own, own), own)]
    c, other = asked[0:1], asked[1:2]
    apart = jnp.where(other >= c, other - c, other - c + count)
    row = jnp.where(apart <= count // 2, apart * count + c, (count - apart) * count + other)
    pick[...] = one_hot_columns(row, pick.shape[0]).astype(BF16)


def pick_kernel(n_col, scale, gathers, place, pick, *refs):
    arrays, (out, found, turned) = refs[: len(gathers)], refs[len(gathers) :]
    me = place[0] // n_col
    whole = jnp.concatenate([array[...] for array in arrays])
    found[...] = jnp.dot(whole, pick[...], preferred_element_type=F32) * scale
    base = 0
    for array, (steps, chunks) in zip(arrays, gathers):
        each = sum(rows for _, rows, _ in chunks)
        for j in range(array.shape[0] // each):
            block = sum((((me ^ j) >> bit) % 2) << s for s, bit in enumerate(steps))
            used = 0
            for start, rows, order in chunks:
                spot = sum(((j >> bit) & 1) << (len(order) - 1 - s) for s, bit in enumerate(order))
                to = start + spot * rows
                turned[to : to + rows, :] = found[pl.ds(base + block * each + used, rows), :]
                used += rows
        base += array.shape[0]
    out[...] = turned[...].T


def swap(x, axis, bits, size):
    return lax.ppermute(x, axis, [(i, i ^ bits) for i in range(size)])


def solution(mesh):
    n_row, n_col = mesh.shape["row"], mesh.shape["col"]
    row_bits, col_bits = n_row.bit_length() - 1, n_col.bit_length() - 1

    def per_device(screened, val_orbitals, con_orbitals, val_pairs, con_pairs):
        own_rows, own_columns = screened.shape
        count, grid = con_orbitals.shape
        n_val = val_orbitals.shape[0]
        blocks = count // 2 + 1
        while blocks * count % 128:
            blocks += 1
        unordered = blocks * count
        n_pairs = val_pairs.shape[0]
        per_col = n_pairs // n_col
        chunks = CHUNKS if n_pairs >= 8 * CHUNKS * n_row * n_col and row_bits == 3 else 1
        width = per_col // chunks
        starts = [k * width for k in range(chunks)]
        place = (lax.axis_index("row") * n_col + lax.axis_index("col")).astype(jnp.int32)[None]
        smem = pl.BlockSpec(memory_space=pltpu.SMEM)
        vmem = pl.BlockSpec(memory_space=pltpu.VMEM)
        anywhere = pl.BlockSpec(memory_space=pl.ANY)
        hbm = pl.BlockSpec(memory_space=pltpu.HBM)

        def params(mib):
            return pltpu.CompilerParams(vmem_limit_bytes=mib << 20)

        def outs(rows):
            return [pltpu.VMEM((rows, unordered), F32), pltpu.VMEM((rows, unordered), BF16)]

        stripe = min(512, own_rows)
        n_stripes = own_rows // stripe
        held = [pltpu.VMEM((stripe, own_columns), BF16)] * n_stripes + [pltpu.VMEM((unordered, own_rows), BF16)]
        hots = [pltpu.VMEM((n_pairs, n_val), BF16)] * 2
        n_held = n_stripes + 1
        arguments = (place, *[pltpu.with_memory_space_constraint(x, pltpu.HBM) for x in (val_pairs.T, val_orbitals, con_orbitals, screened)])
        inputs = [
            pltpu.VMEM((2, n_pairs), jnp.int32),
            pltpu.VMEM((n_val, own_columns), BF16),
            pltpu.VMEM((count, own_rows), BF16),
            pltpu.VMEM((2 * count, min(512, own_rows)), F32),
            pltpu.SemaphoreType.DMA((n_stripes,)),
            pltpu.SemaphoreType.DMA((3,)),
        ]
        n = n_col * width

        def single():
            return pl.pallas_call(
                functools.partial(single_kernel, n_col, n_stripes),
                in_specs=[smem] + [hbm] * 4,
                out_specs=[vmem] * 2,
                out_shape=outs(n // 2),
                scratch_shapes=[pltpu.VMEM((n, own_columns), BF16), pltpu.VMEM((n, unordered), F32), held[-1], *hots, *inputs, *held[:-1]],
                compiler_params=params(40),
                name="single",
            )(*arguments)

        def call(kernel, in_specs, out_shape, operands, after=(), scratch=(), aliases={}, mib=8, flops=0):
            return pl.pallas_call(
                kernel,
                in_specs=in_specs + [anywhere] * len(after),
                out_specs=[vmem] * len(out_shape),
                out_shape=out_shape,
                scratch_shapes=list(scratch),
                input_output_aliases=aliases,
                compiler_params=params(mib),
                cost_estimate=pl.CostEstimate(flops=flops, bytes_accessed=1 << 20, transcendentals=0),
            )(*operands, *after)

        def load():
            kept, *rest = call(
                functools.partial(load_kernel, n_col, starts[3], width, n_stripes),
                [smem] + [hbm] * 4,
                [pltpu.VMEM((width, own_rows), F32)]
                + [pltpu.VMEM((width, own_rows), BF16)] * (n_col - 1)
                + [pltpu.VMEM((2 * n, own_columns), BF16), *held, *hots],
                arguments,
                scratch=[pltpu.VMEM((n, own_columns), BF16), pltpu.VMEM((n, own_rows), F32), *inputs],
                mib=12,
                flops=2 * n * own_rows * own_columns,
            )
            return kept, rest[: n_col - 1], rest[n_col - 1], rest[n_col : n_col + n_held], rest[n_col + n_held :]

        def pair(fixed, val_density, after):
            out = call(
                functools.partial(pair_kernel, n_col, n_stripes, len(after)),
                [smem] + [vmem] * (n_held + 1),
                [outs(n // 2)[0]] * 2 + [outs(n)[1]] + held,
                (place, *fixed, val_density),
                after,
                [pltpu.VMEM((2 * n, unordered), F32)],
                {1 + i: 3 + i for i in range(n_held)},
                12,
                4 * n * own_rows * (own_columns + unordered),
            )
            return list(out[:2]), out[2], list(out[3:])

        def scatter(sent, axis, bits):
            got = []
            for flip, x in enumerate(sent, 1):
                mask = sum(((flip >> (len(bits) - 1 - k)) & 1) << bit for k, bit in enumerate(bits))
                got.append(swap(x, axis, mask, mesh.shape[axis]))
            return got

        def spread(kept, got, axis, bits, eaches, offsets):
            ways = 1 << len(bits)
            rows, minor = [k.shape[0] // ways for k in kept], kept[0].shape[1]
            out = call(
                functools.partial(spread_kernel, n_col, axis, bits, eaches, offsets, len(got)),
                [smem] + [vmem] * (len(kept) + len(got)),
                [pltpu.VMEM((r, minor), F32) for r in rows] + [pltpu.VMEM((sum(rows), minor), BF16)] * (ways - 1),
                (place, *kept, *got),
                scratch=[pltpu.VMEM((max(rows) * ways, minor), F32)],
                mib=6,
            )
            return list(out[: len(kept)]), list(out[len(kept) :])

        def total(kept, got, offsets):
            return call(
                functools.partial(sum_kernel, offsets),
                [vmem] * (len(kept) + len(got)),
                [pltpu.VMEM((sum(k.shape[0] for k in kept), kept[0].shape[1]), BF16)],
                (*kept, *got),
                mib=6,
            )[0]

        def fold(kept, got, targets, got_groups=None, sent_groups=None):
            everything = [list(range(len(kept)))]
            got_groups, sent_groups = got_groups or everything, sent_groups or everything
            rows = [k.shape[0] // (2 if t else 1) for k, t in zip(kept, targets)]
            minor = kept[0].shape[1]
            shapes = [pltpu.VMEM((r, minor), F32) for r, t in zip(rows, targets) if t]
            n_kept = len(shapes)
            shapes += [pltpu.VMEM((sum(rows[c] for c in g), minor), BF16) for g in sent_groups]
            out = pl.pallas_call(
                functools.partial(fold_kernel, n_col, targets, got_groups, sent_groups),
                in_specs=[smem] + [vmem] * (len(kept) + len(got)),
                out_specs=[vmem] * len(shapes),
                out_shape=shapes,
                compiler_params=params(4),
            )(place, *kept, *got)
            return list(out[:n_kept]), list(out[n_kept:])

        order = list(range(1, row_bits))
        orders = [[0] + order for _ in range(chunks)]
        steps = [
            [("row", bit, n_col) for bit in orders[0]] + [("col", bit, n_col >> (bit + 1)) for bit in range(col_bits)] + [None]
        ]
        n_steps = row_bits + col_bits
        sizes = {"row": n_row, "col": n_col}

        def send(k, at, sent):
            axis, bit, _ = steps[k][at]
            return swap(sent, axis, 1 << bit, sizes[axis])

        def run(k, at, until, kept, sent):
            for s in range(at, until):
                got = send(k, s, sent)
                kept, (sent,) = fold(kept, [got], [steps[k][s + 1]] * len(kept))
            return kept, sent

        def gather(part, steps):
            for bits in steps:
                flips = [1 << bits[0]] if len(bits) == 1 else [1 << bits[0], 1 << bits[1], 1 << bits[0] | 1 << bits[1]]
                got = [swap(part, "row", flip, n_row) for flip in flips]
                part = jnp.concatenate([part, *got])
            return part

        if chunks > 1:
            cols = tuple(reversed(range(col_bits)))
            half = n // 2
            b_kept, b_sent, val_a, fixed, hot = load()
            b_got = scatter(b_sent, "col", cols)
            a_kept, a_sent, fixed = pair(fixed, val_a, b_sent)
            a_got = [swap(a_sent, "row", 1, n_row)]
            when = [a_sent]
            val_m = call(
                functools.partial(val_kernel, n_col, starts[2], width, 1), [vmem] * 3,
                [pltpu.VMEM((n, own_columns), BF16)], (*hot, val_orbitals), when, mib=6,
            )[0]
            a_kept, a_sent = spread(a_kept, a_got, "row", tuple(order), [n_col] * 2, [0, half])
            a_got = scatter(a_sent, "row", order)
            t_m = call(
                functools.partial(grid_kernel, n_stripes, len(a_sent)), [vmem] * (n_stripes + 1),
                [pltpu.VMEM((n, own_rows), BF16)], (*fixed[:-1], val_m), a_sent, mib=8, flops=2 * n * own_rows * own_columns,
            )[0]
            t_b = total([b_kept], b_got, [0])
            cut = (unordered // 256 + 1) * 128
            same = [held[-1], pltpu.VMEM(t_m.shape, BF16), pltpu.VMEM(t_b.shape, BF16)]
            operands, parts = [fixed[-1], t_m, t_b], []
            for first, size, name in ((0, cut, "l"), (cut, unordered - cut, "r")):
                again = same if name == "l" else []
                m_kept, b_kept, sent, *operands = call(
                    functools.partial(con_kernel, n_col, first, size, len(again)), [smem] + [vmem] * 3,
                    [pltpu.VMEM((half, size), F32), pltpu.VMEM((width // 2, size), F32), pltpu.VMEM((half + width // 2, size), BF16)] + again,
                    (place, *operands), scratch=[pltpu.VMEM((n + width, size), F32)], mib=10,
                    aliases={1 + i: 3 + i for i in range(len(again))}, flops=2 * (n + width) * own_rows * size,
                )
                parts.append(([m_kept, b_kept], [swap(sent, "row", 1, n_row)]))
            cuts = []
            for name, (kept, got) in zip("lr", parts):
                kept, sent = spread(kept, got, "row", tuple(order), [n_col, 1], [0, half])
                cuts.append((kept, scatter(sent, "row", order)))
            a_kept, a_sent = spread(a_kept, a_got, "col", cols, [1, 1], [0, a_kept[0].shape[0]])
            a_got = scatter(a_sent, "col", cols)
            join = lambda a, b: jnp.concatenate([a, b], axis=1)
            (m_kept, b_kept), mb_got = [[join(a, b) for a, b in zip(*x)] for x in zip(*cuts)]
            rows = m_kept.shape[0]
            m_kept, m_sent = spread([m_kept], mb_got, "col", cols, [1], [0])
            m_got = scatter(m_sent, "col", cols)
            b_sums = total([b_kept], mb_got, [rows])
            a_sums = total(a_kept, a_got, [0, a_kept[0].shape[0]])
            m_sums = total(m_kept, m_got, [0])
            square = [order, [0]]
            arrays = [gather(jnp.concatenate([a_sums, b_sums]), square), gather(m_sums, square)]
            gathers = [(order + [0], [0, 1, 3]), (order + [0], [2])]
        else:
            kept, sent = single()
            when = []
            _, late = run(0, 0, n_steps, [kept], sent)
            late_bits = order[::-1] + [0]
            arrays, gathers = [gather(late, [[bit] for bit in late_bits])], [(late_bits, [0])]
        gathers = [(bits, [(starts[k], width // n_row, orders[k]) for k in ks]) for bits, ks in gathers]

        own = con_pairs.shape[0] // n_row
        pick = pl.pallas_call(
            functools.partial(hot_kernel, n_col, count, len(when)),
            in_specs=[smem, vmem] + [anywhere] * len(when),
            out_specs=vmem,
            out_shape=pltpu.VMEM((unordered, own), BF16),
            compiler_params=params(8),
            name="hot",
        )(place, con_pairs.T, *when)
        return pl.pallas_call(
            functools.partial(pick_kernel, n_col, float(grid ** (-0.5)), gathers),
            in_specs=[smem] + [vmem] * (1 + len(arrays)),
            out_specs=vmem,
            out_shape=jax.ShapeDtypeStruct((own, per_col), F32),
            scratch_shapes=[pltpu.VMEM((per_col, own), F32)] * 2,
            compiler_params=params(20),
            name="pick",
        )(place, pick, *arrays)

    in_specs = (P("row", "col"), P(None, "col"), P(), P(), P())

    return jax.shard_map(per_device, mesh=mesh, in_specs=in_specs, out_specs=P("row", "col"), check_vma=False)
```

```python
import functools

import jax
import jax.numpy as jnp
from jax import lax
from jax.experimental import pallas as pl
from jax.experimental.pallas import tpu as pltpu
from jax.sharding import PartitionSpec as P


CHUNKS = 4

F32, BF16 = jnp.float32, jnp.bfloat16
CONTRACT_MINOR = (((1,), (1,)), ((), ()))


def one_hot_columns(index, count):
    numbers = lax.broadcasted_iota(jnp.int32, (count, index.shape[1]), 0)
    return jnp.where(numbers == index, 1.0, 0.0)


def groups(ref, n_col, start, width):
    each = ref.shape[0] // n_col
    return jnp.concatenate([ref[z * each + start : z * each + start + width, :] for z in range(n_col)])


def build_val(first, second, val_ref, val_density):
    grid = val_ref.shape[1]
    step = min(2048, grid)

    @pl.loop(0, grid // step)
    def _(i):
        at = pl.ds(pl.multiple_of(i * step, step), step)
        orbitals = val_ref[:, at]
        a = jnp.dot(first, orbitals, preferred_element_type=F32)
        b = jnp.dot(second, orbitals, preferred_element_type=F32)
        val_density[:, at] = (a * b).astype(BF16)


def build_con(con, rolled, density):
    count, columns = con.shape
    wide = min(512, columns)
    apart = density.shape[0] // count

    @pl.loop(0, columns // wide)
    def _(i):
        at = pl.ds(pl.multiple_of(i * wide, wide), wide)
        one = con[:, at].astype(F32)
        for shift in range(8):
            moved = one if shift == 0 else jnp.concatenate([one[shift:], one[:shift]])
            rolled[0:count, :] = moved
            rolled[count : 2 * count, :] = moved
            for d in range(shift, apart, 8):
                other = rolled[d - shift : d - shift + count, :]
                density[d * count : (d + 1) * count, at] = (one * other).astype(BF16)


def product(numbers, w, density, val_density):
    stripe = w[0].shape[0]
    t = [lax.dot_general(val_density[...], w[s][...], CONTRACT_MINOR, preferred_element_type=F32).astype(BF16) for s in numbers]
    rows = slice(numbers[0] * stripe, (numbers[-1] + 1) * stripe)
    return lax.dot_general(jnp.concatenate(t, axis=1), density[:, rows], CONTRACT_MINOR, preferred_element_type=F32)


def hand_out(n_col, mine, acc, kept, sent):
    half = kept[0].shape[0] // n_col
    for c, own in enumerate(kept):
        for z in range(n_col):
            first = (z * len(kept) + c) * 2
            to = slice(z * half, (z + 1) * half)
            own[to, :] = acc[pl.ds(pl.multiple_of((first + mine) * half, half), half), :]
            to = slice((c * n_col + z) * half, (c * n_col + z + 1) * half)
            sent[to, :] = acc[pl.ds(pl.multiple_of((first + 1 - mine) * half, half), half), :].astype(BF16)


def deal(index, ways, each, size, source, base, outs, starts):
    for flip, (out, start) in enumerate(zip(outs, starts)):
        for g in range(each):
            at = base + g * ways * size + (index ^ flip) * size
            rows = source[pl.ds(pl.multiple_of(at, size), size), :]
            out[start + g * size : start + (g + 1) * size, :] = rows.astype(out.dtype)


def fetch_all(n_col, n_stripes, place, hbm, vmem, sems, in_sems):
    pairs, val, con_all, w_hbm = hbm
    pairs_here, val_here, con, w = vmem
    columns, stripe = con.shape[1], w[0].shape[0]
    mine = pl.ds(pl.multiple_of((place[0] // n_col) * columns, columns), columns)
    fetches = [
        pltpu.make_async_copy(pairs, pairs_here, in_sems.at[0]),
        pltpu.make_async_copy(val, val_here, in_sems.at[1]),
        pltpu.make_async_copy(con_all.at[:, mine], con, in_sems.at[2]),
    ]
    fetches += [
        pltpu.make_async_copy(w_hbm.at[pl.ds(s * stripe, stripe), :], w[s], sems.at[s]) for s in range(n_stripes)
    ]
    for fetch in fetches[:3]:
        fetch.start()
    return fetches[:3], fetches[3:]


def make_hot(pairs, hot1, hot2):
    hot1[...] = one_hot_columns(pairs[0:1, :], hot1.shape[1]).T.astype(BF16)
    hot2[...] = one_hot_columns(pairs[1:2, :], hot2.shape[1]).T.astype(BF16)


def single_kernel(n_col, n_stripes, place, pairs, val, con_all, w_hbm, kept, sent, val_density, acc, density, hot1, hot2, pairs_here, val_here, con, rolled, sems, in_sems, *w):
    inputs, stripes = fetch_all(n_col, n_stripes, place, (pairs, val, con_all, w_hbm), (pairs_here, val_here, con, w), sems, in_sems)
    for fetch in stripes:
        fetch.start()
    for fetch in inputs:
        fetch.wait()
    make_hot(pairs_here, hot1, hot2)
    build_val(hot1[...], hot2[...], val_here, val_density)
    build_con(con, rolled, density)
    for fetch in stripes:
        fetch.wait()
    acc[...] = product(list(range(n_stripes)), w, density, val_density)
    hand_out(n_col, place[0] // n_col % 2, acc, [kept], sent)


def load_kernel(n_col, start, width, n_stripes, place, pairs, val, con_all, w_hbm, kept, *refs):
    sent, (val_a, *refs) = refs[: n_col - 1], refs[n_col - 1 :]
    w, refs = refs[:n_stripes], refs[n_stripes:]
    density, hot1, hot2, val_b, acc, pairs_here, val_here, con, rolled, sems, in_sems = refs
    inputs, stripes = fetch_all(n_col, n_stripes, place, (pairs, val, con_all, w_hbm), (pairs_here, val_here, con, w), sems, in_sems)
    inputs[0].wait()
    inputs[1].wait()
    for fetch in stripes:
        fetch.start()
    make_hot(pairs_here, hot1, hot2)
    build_val(groups(hot1, n_col, start, width), groups(hot2, n_col, start, width), val_here, val_b)
    build_val(groups(hot1, n_col, 0, 2 * width), groups(hot2, n_col, 0, 2 * width), val_here, val_a)
    inputs[2].wait()
    build_con(con, rolled, density)
    for s, fetch in enumerate(stripes):
        fetch.wait()
        stripe = w[s].shape[0]
        t = lax.dot_general(val_b[...], w[s][...], CONTRACT_MINOR, preferred_element_type=F32)
        acc[:, s * stripe : (s + 1) * stripe] = t
    deal(place[0] % n_col, n_col, 1, width, acc, 0, [kept, *sent], [0] * n_col)


def pair_kernel(n_col, n_stripes, n_after, place, *refs):
    w, refs = refs[:n_stripes], refs[n_stripes:]
    (density, val_density), refs = refs[:2], refs[2 + n_after :]
    kept, sent, acc = refs[:2], refs[2], refs[-1]
    at_once = 2 - n_stripes % 2
    for s in range(0, n_stripes, at_once):
        part = product(list(range(s, s + at_once)), w, density, val_density)
        if s == 0:
            acc[...] = part
        else:
            acc[...] += part
    hand_out(n_col, place[0] // n_col % 2, acc, kept, sent)


def val_kernel(n_col, start, width, n_after, hot1, hot2, val, *refs):
    build_val(groups(hot1, n_col, start, width), groups(hot2, n_col, start, width), val, refs[n_after])


def grid_kernel(n_stripes, n_after, *refs):
    w, val_density, t = refs[:n_stripes], refs[n_stripes], refs[n_stripes + 1 + n_after]
    stripe = w[0].shape[0]
    for s in range(n_stripes):
        part = lax.dot_general(val_density[...], w[s][...], CONTRACT_MINOR, preferred_element_type=F32)
        t[:, s * stripe : (s + 1) * stripe] = part.astype(BF16)


def con_kernel(n_col, first, size_of_cut, n_same, place, density, t_m, t_b, kept_m, kept_b, sent, *refs):
    acc = refs[n_same]
    both = jnp.concatenate([t_m[...], t_b[...]])
    rows_of_cut = density[first : first + size_of_cut, :]
    acc[...] = lax.dot_general(both, rows_of_cut, CONTRACT_MINOR, preferred_element_type=F32)
    mine = place[0] // n_col % 2
    rows, size = t_m.shape[0], t_b.shape[0] // 2
    deal(mine, 2, n_col, size, acc, 0, [kept_m, sent], [0, 0])
    deal(mine, 2, 1, size, acc, rows, [kept_b, sent], [0, rows // 2])


def spread_kernel(n_col, axis, bits, eaches, offsets, n_got, place, *refs):
    n, ways = len(eaches), 1 << len(bits)
    kept, got, refs = refs[:n], refs[n : n + n_got], refs[n + n_got :]
    kept_out, sent, part = refs[:n], refs[n:-1], refs[-1]
    me = place[0] // n_col if axis == "row" else place[0] % n_col
    index = sum(((me >> bit) & 1) << (len(bits) - 1 - k) for k, bit in enumerate(bits))
    to = 0
    for c, (each, at) in enumerate(zip(eaches, offsets)):
        rows = kept[c].shape[0]
        total = kept[c][...]
        for arrived in got:
            total = total + arrived[at : at + rows, :].astype(F32)
        part[0:rows, :] = total
        deal(index, ways, each, rows // ways // each, part, 0, [kept_out[c], *sent], [0] + [to] * (ways - 1))
        to += rows // ways


def sum_kernel(offsets, *refs):
    kept, got, out = refs[: len(offsets)], refs[len(offsets) : -1], refs[-1]
    to = 0
    for part, at in zip(kept, offsets):
        rows = part.shape[0]
        total = part[...]
        for arrived in got:
            total = total + arrived[at : at + rows, :].astype(F32)
        out[to : to + rows, :] = total.astype(BF16)
        to += rows


def fold_kernel(n_col, targets, got_groups, sent_groups, place, *refs):
    n = len(targets)
    kept, got = refs[:n], refs[n : n + len(got_groups)]
    out = refs[n + len(got_groups) :]
    halves, sent = out[: len(out) - len(sent_groups)], out[len(out) - len(sent_groups) :]
    source, sink = {}, {}
    for array, group in zip(got, got_groups):
        at = 0
        for c in group:
            source.setdefault(c, []).append((array, at))
            at += kept[c].shape[0]
    for array, group in zip(sent, sent_groups):
        at = 0
        for c in group:
            sink[c] = array, at
            at += kept[c].shape[0] // (2 if targets[c] else 1)
    for c, target in enumerate(targets):
        rows, (other, to) = kept[c].shape[0], sink[c]

        def part(first, size, c=c):
            total = kept[c][first : first + size, :]
            for array, at in source[c]:
                total = total + array[at + first : at + first + size, :].astype(F32)
            return total

        if target is None:
            other[to : to + rows, :] = part(0, rows).astype(BF16)
            continue
        axis, bit, each = target
        me = place[0] // n_col if axis == "row" else place[0] % n_col
        high = (me >> bit) % 2 == 1
        half = rows // each // 2
        for z in range(each):
            a, b = 2 * z * half, (2 * z + 1) * half
            low_part, high_part = part(a, half), part(b, half)
            halves[c][z * half : (z + 1) * half, :] = jnp.where(high, high_part, low_part)
            other[to + z * half : to + (z + 1) * half, :] = jnp.where(high, low_part, high_part).astype(BF16)


def hot_kernel(n_col, count, n_after, place, pairs, *refs):
    pick = refs[n_after]
    own = pick.shape[1]
    me = place[0] // n_col
    if own % 128:
        every = pairs[...]
        asked = functools.reduce(
            lambda a, i: jnp.where(me == i, every[:, i * own : (i + 1) * own], a), range(pairs.shape[1] // own), every[:, :own]
        )
    else:
        asked = pairs[:, pl.ds(pl.multiple_of(me * own, own), own)]
    c, other = asked[0:1], asked[1:2]
    apart = jnp.where(other >= c, other - c, other - c + count)
    row = jnp.where(apart <= count // 2, apart * count + c, (count - apart) * count + other)
    pick[...] = one_hot_columns(row, pick.shape[0]).astype(BF16)


def pick_kernel(n_col, scale, gathers, place, pick, *refs):
    arrays, (out, found, turned, done, sems) = refs[: len(gathers)], refs[len(gathers) :]
    me = place[0] // n_col
    whole = jnp.concatenate([array[...] for array in arrays])
    own = done.shape[0]
    pieces = 2 if own % 256 == 0 else 1
    size = own // pieces
    copies = []
    for piece in range(pieces):
        at = slice(piece * size, (piece + 1) * size)
        found[:, at] = jnp.dot(whole, pick[:, at], preferred_element_type=F32) * scale
        base = 0
        for array, (steps, chunks) in zip(arrays, gathers):
            each = sum(rows for _, rows, _ in chunks)
            for j in range(array.shape[0] // each):
                block = sum((((me ^ j) >> bit) % 2) << s for s, bit in enumerate(steps))
                used = 0
                for start, rows, order in chunks:
                    spot = sum(((j >> bit) & 1) << (len(order) - 1 - s) for s, bit in enumerate(order))
                    to = start + spot * rows
                    turned[to : to + rows, at] = found[pl.ds(base + block * each + used, rows), at]
                    used += rows
            base += array.shape[0]
        done[at, :] = turned[:, at].T
        rows = pl.ds(piece * size, size)
        copies.append(pltpu.make_async_copy(done.at[rows, :], out.at[rows, :], sems.at[piece]))
        copies[-1].start()
    for copy in copies:
        copy.wait()


def swap(x, axis, bits, size):
    return lax.ppermute(x, axis, [(i, i ^ bits) for i in range(size)])


def solution(mesh):
    n_row, n_col = mesh.shape["row"], mesh.shape["col"]
    row_bits, col_bits = n_row.bit_length() - 1, n_col.bit_length() - 1

    def per_device(screened, val_orbitals, con_orbitals, val_pairs, con_pairs):
        own_rows, own_columns = screened.shape
        count, grid = con_orbitals.shape
        n_val = val_orbitals.shape[0]
        blocks = count // 2 + 1
        while blocks * count % 128:
            blocks += 1
        unordered = blocks * count
        n_pairs = val_pairs.shape[0]
        per_col = n_pairs // n_col
        chunks = CHUNKS if n_pairs >= 8 * CHUNKS * n_row * n_col and row_bits == 3 else 1
        width = per_col // chunks
        starts = [k * width for k in range(chunks)]
        place = (lax.axis_index("row") * n_col + lax.axis_index("col")).astype(jnp.int32)[None]
        smem = pl.BlockSpec(memory_space=pltpu.SMEM)
        vmem = pl.BlockSpec(memory_space=pltpu.VMEM)
        anywhere = pl.BlockSpec(memory_space=pl.ANY)
        hbm = pl.BlockSpec(memory_space=pltpu.HBM)

        def params(mib):
            return pltpu.CompilerParams(vmem_limit_bytes=mib << 20)

        def outs(rows):
            return [pltpu.VMEM((rows, unordered), F32), pltpu.VMEM((rows, unordered), BF16)]

        stripe = min(512, own_rows)
        n_stripes = own_rows // stripe
        held = [pltpu.VMEM((stripe, own_columns), BF16)] * n_stripes + [pltpu.VMEM((unordered, own_rows), BF16)]
        hots = [pltpu.VMEM((n_pairs, n_val), BF16)] * 2
        n_held = n_stripes + 1
        arguments = (place, *[pltpu.with_memory_space_constraint(x, pltpu.HBM) for x in (val_pairs.T, val_orbitals, con_orbitals, screened)])
        inputs = [
            pltpu.VMEM((2, n_pairs), jnp.int32),
            pltpu.VMEM((n_val, own_columns), BF16),
            pltpu.VMEM((count, own_rows), BF16),
            pltpu.VMEM((2 * count, min(512, own_rows)), F32),
            pltpu.SemaphoreType.DMA((n_stripes,)),
            pltpu.SemaphoreType.DMA((3,)),
        ]
        n = n_col * width

        def single():
            return pl.pallas_call(
                functools.partial(single_kernel, n_col, n_stripes),
                in_specs=[smem] + [hbm] * 4,
                out_specs=[vmem] * 2,
                out_shape=outs(n // 2),
                scratch_shapes=[pltpu.VMEM((n, own_columns), BF16), pltpu.VMEM((n, unordered), F32), held[-1], *hots, *inputs, *held[:-1]],
                compiler_params=params(40),
                name="single",
            )(*arguments)

        def call(kernel, in_specs, out_shape, operands, after=(), scratch=(), aliases={}, mib=8, flops=0):
            return pl.pallas_call(
                kernel,
                in_specs=in_specs + [anywhere] * len(after),
                out_specs=[vmem] * len(out_shape),
                out_shape=out_shape,
                scratch_shapes=list(scratch),
                input_output_aliases=aliases,
                compiler_params=params(mib),
                cost_estimate=pl.CostEstimate(flops=flops, bytes_accessed=1 << 20, transcendentals=0),
            )(*operands, *after)

        def load():
            kept, *rest = call(
                functools.partial(load_kernel, n_col, starts[3], width, n_stripes),
                [smem] + [hbm] * 4,
                [pltpu.VMEM((width, own_rows), F32)]
                + [pltpu.VMEM((width, own_rows), BF16)] * (n_col - 1)
                + [pltpu.VMEM((2 * n, own_columns), BF16), *held, *hots],
                arguments,
                scratch=[pltpu.VMEM((n, own_columns), BF16), pltpu.VMEM((n, own_rows), F32), *inputs],
                mib=12,
                flops=2 * n * own_rows * own_columns,
            )
            return kept, rest[: n_col - 1], rest[n_col - 1], rest[n_col : n_col + n_held], rest[n_col + n_held :]

        def pair(fixed, val_density, after):
            out = call(
                functools.partial(pair_kernel, n_col, n_stripes, len(after)),
                [smem] + [vmem] * (n_held + 1),
                [outs(n // 2)[0]] * 2 + [outs(n)[1]] + held,
                (place, *fixed, val_density),
                after,
                [pltpu.VMEM((2 * n, unordered), F32)],
                {1 + i: 3 + i for i in range(n_held)},
                12,
                4 * n * own_rows * (own_columns + unordered),
            )
            return list(out[:2]), out[2], list(out[3:])

        def scatter(sent, axis, bits):
            got = []
            for flip, x in enumerate(sent, 1):
                mask = sum(((flip >> (len(bits) - 1 - k)) & 1) << bit for k, bit in enumerate(bits))
                got.append(swap(x, axis, mask, mesh.shape[axis]))
            return got

        def spread(kept, got, axis, bits, eaches, offsets):
            ways = 1 << len(bits)
            rows, minor = [k.shape[0] // ways for k in kept], kept[0].shape[1]
            out = call(
                functools.partial(spread_kernel, n_col, axis, bits, eaches, offsets, len(got)),
                [smem] + [vmem] * (len(kept) + len(got)),
                [pltpu.VMEM((r, minor), F32) for r in rows] + [pltpu.VMEM((sum(rows), minor), BF16)] * (ways - 1),
                (place, *kept, *got),
                scratch=[pltpu.VMEM((max(rows) * ways, minor), F32)],
                mib=6,
            )
            return list(out[: len(kept)]), list(out[len(kept) :])

        def total(kept, got, offsets):
            return call(
                functools.partial(sum_kernel, offsets),
                [vmem] * (len(kept) + len(got)),
                [pltpu.VMEM((sum(k.shape[0] for k in kept), kept[0].shape[1]), BF16)],
                (*kept, *got),
                mib=6,
            )[0]

        def fold(kept, got, targets, got_groups=None, sent_groups=None):
            everything = [list(range(len(kept)))]
            got_groups, sent_groups = got_groups or everything, sent_groups or everything
            rows = [k.shape[0] // (2 if t else 1) for k, t in zip(kept, targets)]
            minor = kept[0].shape[1]
            shapes = [pltpu.VMEM((r, minor), F32) for r, t in zip(rows, targets) if t]
            n_kept = len(shapes)
            shapes += [pltpu.VMEM((sum(rows[c] for c in g), minor), BF16) for g in sent_groups]
            out = pl.pallas_call(
                functools.partial(fold_kernel, n_col, targets, got_groups, sent_groups),
                in_specs=[smem] + [vmem] * (len(kept) + len(got)),
                out_specs=[vmem] * len(shapes),
                out_shape=shapes,
                compiler_params=params(4),
            )(place, *kept, *got)
            return list(out[:n_kept]), list(out[n_kept:])

        order = list(range(1, row_bits))
        orders = [[0] + order for _ in range(chunks)]
        steps = [
            [("row", bit, n_col) for bit in orders[0]] + [("col", bit, n_col >> (bit + 1)) for bit in range(col_bits)] + [None]
        ]
        n_steps = row_bits + col_bits
        sizes = {"row": n_row, "col": n_col}

        def send(k, at, sent):
            axis, bit, _ = steps[k][at]
            return swap(sent, axis, 1 << bit, sizes[axis])

        def run(k, at, until, kept, sent):
            for s in range(at, until):
                got = send(k, s, sent)
                kept, (sent,) = fold(kept, [got], [steps[k][s + 1]] * len(kept))
            return kept, sent

        def gather(part, steps):
            for bits in steps:
                flips = [1 << bits[0]] if len(bits) == 1 else [1 << bits[0], 1 << bits[1], 1 << bits[0] | 1 << bits[1]]
                got = [swap(part, "row", flip, n_row) for flip in flips]
                part = jnp.concatenate([part, *got])
            return part

        if chunks > 1:
            cols = tuple(reversed(range(col_bits)))
            half = n // 2
            b_kept, b_sent, val_a, fixed, hot = load()
            b_got = scatter(b_sent, "col", cols)
            a_kept, a_sent, fixed = pair(fixed, val_a, b_sent)
            a_got = [swap(a_sent, "row", 1, n_row)]
            when = [a_sent]
            val_m = call(
                functools.partial(val_kernel, n_col, starts[2], width, 1), [vmem] * 3,
                [pltpu.VMEM((n, own_columns), BF16)], (*hot, val_orbitals), when, mib=6,
            )[0]
            a_kept, a_sent = spread(a_kept, a_got, "row", tuple(order), [n_col] * 2, [0, half])
            a_got = scatter(a_sent, "row", order)
            t_m = call(
                functools.partial(grid_kernel, n_stripes, len(a_sent)), [vmem] * (n_stripes + 1),
                [pltpu.VMEM((n, own_rows), BF16)], (*fixed[:-1], val_m), a_sent, mib=8, flops=2 * n * own_rows * own_columns,
            )[0]
            t_b = total([b_kept], b_got, [0])
            cut = (unordered // 256 + 1) * 128
            same = [held[-1], pltpu.VMEM(t_m.shape, BF16), pltpu.VMEM(t_b.shape, BF16)]
            operands, parts = [fixed[-1], t_m, t_b], []
            for first, size, name in ((0, cut, "l"), (cut, unordered - cut, "r")):
                again = same if name == "l" else []
                m_kept, b_kept, sent, *operands = call(
                    functools.partial(con_kernel, n_col, first, size, len(again)), [smem] + [vmem] * 3,
                    [pltpu.VMEM((half, size), F32), pltpu.VMEM((width // 2, size), F32), pltpu.VMEM((half + width // 2, size), BF16)] + again,
                    (place, *operands), scratch=[pltpu.VMEM((n + width, size), F32)], mib=10,
                    aliases={1 + i: 3 + i for i in range(len(again))}, flops=2 * (n + width) * own_rows * size,
                )
                parts.append(([m_kept, b_kept], [swap(sent, "row", 1, n_row)]))
            cuts = []
            for name, (kept, got) in zip("lr", parts):
                kept, sent = spread(kept, got, "row", tuple(order), [n_col, 1], [0, half])
                cuts.append((kept, scatter(sent, "row", order)))
            a_kept, a_sent = spread(a_kept, a_got, "col", cols, [1, 1], [0, a_kept[0].shape[0]])
            a_got = scatter(a_sent, "col", cols)
            join = lambda a, b: jnp.concatenate([a, b], axis=1)
            (m_kept, b_kept), mb_got = [[join(a, b) for a, b in zip(*x)] for x in zip(*cuts)]
            rows = m_kept.shape[0]
            m_kept, m_sent = spread([m_kept], mb_got, "col", cols, [1], [0])
            m_got = scatter(m_sent, "col", cols)
            b_sums = total([b_kept], mb_got, [rows])
            a_sums = total(a_kept, a_got, [0, a_kept[0].shape[0]])
            m_sums = total(m_kept, m_got, [0])
            square = [order, [0]]
            arrays = [gather(jnp.concatenate([a_sums, b_sums]), square), gather(m_sums, square)]
            gathers = [(order + [0], [0, 1, 3]), (order + [0], [2])]
        else:
            kept, sent = single()
            when = []
            _, late = run(0, 0, n_steps, [kept], sent)
            late_bits = order[::-1] + [0]
            arrays, gathers = [gather(late, [[bit] for bit in late_bits])], [(late_bits, [0])]
        gathers = [(bits, [(starts[k], width // n_row, orders[k]) for k in ks]) for bits, ks in gathers]

        own = con_pairs.shape[0] // n_row
        pick = pl.pallas_call(
            functools.partial(hot_kernel, n_col, count, len(when)),
            in_specs=[smem, vmem] + [anywhere] * len(when),
            out_specs=vmem,
            out_shape=pltpu.VMEM((unordered, own), BF16),
            compiler_params=params(8),
            name="hot",
        )(place, con_pairs.T, *when)
        return pl.pallas_call(
            functools.partial(pick_kernel, n_col, float(grid ** (-0.5)), gathers),
            in_specs=[smem] + [vmem] * (1 + len(arrays)),
            out_specs=anywhere,
            out_shape=jax.ShapeDtypeStruct((own, per_col), F32),
            scratch_shapes=[pltpu.VMEM((per_col, own), F32)] * 2
            + [pltpu.VMEM((own, per_col), F32), pltpu.SemaphoreType.DMA((2,))],
            compiler_params=params(20),
            name="pick",
        )(place, pick, *arrays)

    in_specs = (P("row", "col"), P(None, "col"), P(), P(), P())

    return jax.shard_map(per_device, mesh=mesh, in_specs=in_specs, out_specs=P("row", "col"), check_vma=False)
```
